128 devices in a mesh: ep: 64 (over z, y, x), dp: 2 (over core).
Axes of the slice: x: 4, y: 4, z: 4, core: 2. Of those that a mesh axis runs over, the one named last changes fastest.
Arguments:
- residual: bfloat16 [9216, 2048], P(('ep', 'dp')), may hold values from -6 to 6
- queries: bfloat16 [9216, 4096], P('ep', 'dp'), may hold values from -4.5 to 4.5
- fresh_rotated_keys: bfloat16 [9216, 512], P('ep', 'dp'), may hold values from -6 to 6
- fresh_values: bfloat16 [9216, 512], P('ep', 'dp'), may hold values from -6 to 6
- cache_keys: bfloat16 [1088, 256, 512], P('ep', None, 'dp'), may hold values from -4.5 to 4.5
- request_value_cache: bfloat16 [1088, 256, 512], P('ep', None, 'dp'), may hold values from -6 to 6
- cache_lengths: int32 [1088], P('ep'), may hold values from 2 to 256, as said below
- out_proj: bfloat16 [4096, 2048], P('dp'), may hold values from -0.09375 to 0.09375
- router_weight: bfloat16 [2048, 128], replicated, may hold values from -0.125 to 0.125
- norm_gain: bfloat16 [2048], replicated, may hold values from 0.099609375 to 1.8984375
- expert_ids: int32 [9216, 8], P(('ep', 'dp')), may hold values from 0 to 127, all different within a row; in each aligned block of 72 rows (0 to 71, 72 to 143, ...) at most 9 rows name the same one
- live_mask: int32 [9216], P(('ep', 'dp')), may hold values from 0 to 1, as said below
- w_gate: bfloat16 [128, 2048, 768], P(('ep', 'dp')), may hold values from -0.125 to 0.125
- w_up: bfloat16 [128, 2048, 768], P(('ep', 'dp')), may hold values from -0.125 to 0.125
- w_down: bfloat16 [128, 768, 2048], P(('ep', 'dp')), may hold values from -0.21875 to 0.21875
Outputs:
- layer_out: bfloat16 [9216, 2048], P(('ep', 'dp'))
The draws below stay inside these ranges and needn't reach their ends.
Inputs may be any that keep to these rules, and one draw needn't show every extreme that they name: `expert_ids`: in each aligned block of 72 rows (the rows of one device) no expert is named by more than 9 rows. `cache_lengths`: some request has exactly 256 filled slots. `live_mask`: the first 128 rows of a group are all live or all 0.
All inputs are finite; a program needn't handle non-finite values.
Results may differ from the reference program's by a relative error of at most 0.004.
Values may be sent and summed in bfloat16 or wider, within the bound.
No kernel may reach another device: no remote copies, remote signals or barrier semaphores. Data moves between devices by JAX's collectives and lax.ppermute only.
A program may use at most 128 MiB of HBM per device.

```python
import math
import jax
import jax.numpy as jnp
import numpy as np
from jax import lax

D = 2048
QUERY_HEADS = 32
KEY_VALUE_HEADS = 4
HEAD_SIZE = 128
FF = 768
TOPK = 8
PREFILL_ROWS = 128
DECODE_REQUESTS = 16
CACHE_SLOTS_PER = 256
SLOT = 144
TOK_DEV = 72
TOKEN_ROWS = 9216
REQUEST_TOTAL = 1088
EXPERTS = 128
CAPE = 9


def draw_queries(key, part):
    key_start = jax.random.fold_in(key, 11)
    value_tensor = jnp.clip(jax.random.normal(key_start, (TOKEN_ROWS, QUERY_HEADS * HEAD_SIZE), jnp.float32), -4.5, 4.5)
    return value_tensor.astype(jnp.bfloat16)


def draw_cache_keys(key, part):
    key_start = jax.random.fold_in(key, 13)
    value_tensor = jnp.clip(jax.random.normal(key_start, (REQUEST_TOTAL, CACHE_SLOTS_PER, KEY_VALUE_HEADS * HEAD_SIZE), jnp.float32), -4.5, 4.5)
    return value_tensor.astype(jnp.bfloat16)


def draw_cache_lengths(key, part):
    drawn = jax.random.randint(jax.random.fold_in(key, 3), (REQUEST_TOTAL,), 2, CACHE_SLOTS_PER + 1)
    return drawn.at[0].set(CACHE_SLOTS_PER).astype(jnp.int32)


def draw_live_mask(key, part):
    groups = TOKEN_ROWS // SLOT
    shuffled = jax.random.permutation(jax.random.fold_in(key, 5), groups)
    span_live = (shuffled < max(1, groups // 8)).astype(jnp.int32)
    decode_live = (jax.random.randint(jax.random.fold_in(key, 6), (groups, DECODE_REQUESTS), 0, 8) < 7).astype(jnp.int32)
    live_table = jnp.concatenate([jnp.broadcast_to(span_live[:, None], (groups, PREFILL_ROWS)), decode_live], 1)
    return live_table.reshape(TOKEN_ROWS)


def shard_levels(own_key, shape, shards, least, top_value):
    factor_of, own = 1.0, jax.random.fold_in(own_key, 6)
    for dim, blocks in shards:
        draws = jnp.exp(jax.random.uniform(jax.random.fold_in(own, dim), (blocks,), jnp.float32, least / len(shards), top_value / len(shards)))
        factor_of = factor_of * jnp.repeat(draws, shape[dim] // blocks).reshape([-1 if axis == dim else 1 for axis in range(len(shape))])
    return factor_of


def shared_out(stream_key, own, number, rows, number_of, top, most, skew):
    sequence = jax.random.permutation(stream_key, number_of)
    heavy_load, usual = portions_of(number_of, rows * top, most, skew, True), portions_of(number_of, rows * top, most, skew, False)
    places = jnp.arange(number_of)

    def named(sizes, rotation):
        used = int((sizes > 0).sum())
        fixed = max(1, used // 4)
        passed = fixed + (places - fixed + rotation * (used - fixed)) % max(1, number_of - fixed)
        return jnp.zeros((number_of,), jnp.int32).at[sequence[jnp.where(places < fixed, places, passed)]].set(jnp.asarray(sizes, jnp.int32))

    sizes = jnp.where(number % 4 == 0, named(heavy_load, number // 4), named(usual, number - number // 4 - 1))
    mixed = jax.random.permutation(jax.random.fold_in(own, 3), number_of)
    donor, sink = mixed[0:number_of // 2 * 2:2], mixed[1:number_of // 2 * 2:2]
    room = jnp.minimum(sizes[donor] - 1, most - sizes[sink]) // 2
    room = jnp.where((donor == sequence[0]) | (sink == sequence[0]) | (sizes[sink] == 0), 0, jnp.maximum(room, 0))
    passed = jax.random.randint(jax.random.fold_in(own, 4), (number_of // 2,), 0, 1 << 20) % (room + 1)
    sizes = sizes.at[donor].add(-passed).at[sink].add(passed)
    items = jnp.searchsorted(jnp.cumsum(sizes), jnp.arange(rows * top), side="right").astype(jnp.int32)
    grid = items.reshape(top, rows).T
    grid = grid[jax.random.permutation(jax.random.fold_in(own, 1), rows)]
    rotation = jax.random.randint(jax.random.fold_in(own, 2), (rows, 1), 0, top)
    return jnp.take_along_axis(grid, (jnp.arange(top)[None, :] + rotation) % top, axis=1)


def portions_of(amount, total, bound, slope, full):
    weights = [(1 << 20) // math.isqrt(rank ** slope) + 1 for rank in range(1, amount + 1)]
    largest = bound if full else min(bound, max(-(-total // amount), total * weights[0] // sum(weights)))
    least = 1 if total - largest >= amount - 1 else 0
    holding, rest = [largest] + [least] * (amount - 1), total - largest - least * (amount - 1)
    while rest > 0:
        free = [i for i in range(1, amount) if holding[i] < largest] or [i for i in range(1, amount) if holding[i] < bound]
        pool, remaining = sum([weights[i] for i in free]), rest
        for i in free:
            addition = min(bound - holding[i], max(1, remaining * weights[i] // pool), rest)
            holding[i] = holding[i] + addition
            rest = rest - addition
    return np.array(holding)


def noise(own_key, extent, scale, reach, split=(), kind=jnp.bfloat16):
    loudness = shard_levels(own_key, extent, split, -0.22, 0.18) if split else 1.0
    values = jax.random.normal(own_key, extent, jnp.float32) * scale * loudness
    return jnp.minimum(jnp.maximum(values, -reach), reach).astype(kind)


def setup_inputs(seed: int = 0) -> dict:
    arg_keys = jax.random.split(jax.random.key(seed), 16)
    residual = noise(arg_keys[0], (TOKEN_ROWS, D), 1.0, 6.0, ((0, 128),))
    queries = draw_queries(jax.random.fold_in(arg_keys[15], 71), 0)
    fresh_rotated_keys = noise(arg_keys[2], (TOKEN_ROWS, KEY_VALUE_HEADS * HEAD_SIZE), 1.0, 6.0, ((0, 64), (1, 2)))
    fresh_values = noise(arg_keys[3], (TOKEN_ROWS, KEY_VALUE_HEADS * HEAD_SIZE), 1.0, 6.0, ((0, 64), (1, 2)))
    cache_keys = draw_cache_keys(jax.random.fold_in(arg_keys[15], 71), 0)
    request_value_cache = noise(arg_keys[5], (REQUEST_TOTAL, CACHE_SLOTS_PER, KEY_VALUE_HEADS * HEAD_SIZE), 1.0, 6.0, ((0, 64), (2, 2)))
    cache_lengths = draw_cache_lengths(jax.random.fold_in(arg_keys[15], 71), 0)
    out_proj = noise(arg_keys[7], (QUERY_HEADS * HEAD_SIZE, D), (QUERY_HEADS * HEAD_SIZE) ** -0.5, 0.09375, ((0, 2),))
    router_weight = noise(arg_keys[8], (D, EXPERTS), D ** -0.5, 0.125)
    norm_gain = jnp.clip(1.0 + 0.18 * jax.random.normal(arg_keys[9], (D,), jnp.float32), 0.099609375, 1.8984375).astype(jnp.bfloat16)
    expert_ids_keys = jax.random.split(jax.random.fold_in(arg_keys[10], 1), TOKEN_ROWS // TOK_DEV)
    expert_ids_turns = jax.random.permutation(jax.random.fold_in(arg_keys[10], 3), TOKEN_ROWS // TOK_DEV)
    expert_ids = jax.vmap(lambda own, number: shared_out(jax.random.fold_in(arg_keys[10], 2), own, number, TOK_DEV, EXPERTS, TOPK, CAPE, 2))(expert_ids_keys, expert_ids_turns).reshape((TOKEN_ROWS, TOPK))
    live_mask = draw_live_mask(jax.random.fold_in(arg_keys[15], 71), 0)
    w_gate = noise(arg_keys[12], (EXPERTS, D, FF), D ** -0.5, 0.125, ((0, 128),))
    w_up = noise(arg_keys[13], (EXPERTS, D, FF), D ** -0.5, 0.125, ((0, 128),))
    w_down = noise(arg_keys[14], (EXPERTS, FF, D), FF ** -0.5, 0.21875, ((0, 128),))
    return dict(residual=residual, queries=queries, fresh_rotated_keys=fresh_rotated_keys, fresh_values=fresh_values, cache_keys=cache_keys, request_value_cache=request_value_cache, cache_lengths=cache_lengths, out_proj=out_proj, router_weight=router_weight, norm_gain=norm_gain, expert_ids=expert_ids, live_mask=live_mask, w_gate=w_gate, w_up=w_up, w_down=w_down)


NEG_FILL = -1e+30
NORM_EPS = 1e-06

def softmax_rows(scores):
    row_top = lax.optimization_barrier(jnp.max(scores, -1, keepdims=True))
    raised = jnp.exp(scores - row_top)
    return (raised / lax.optimization_barrier(jnp.sum(raised, -1, keepdims=True))).astype(jnp.bfloat16)

def group_attention(query_row_block, key_row_block, value_row_block, stored_keys, stored_values, lengths):
    group_length = QUERY_HEADS // KEY_VALUE_HEADS
    score_scale = 1.0 / math.sqrt(HEAD_SIZE)
    window_query = query_row_block[:PREFILL_ROWS].reshape(PREFILL_ROWS, KEY_VALUE_HEADS, group_length, HEAD_SIZE).astype(jnp.float32)
    window_keys = jnp.concatenate([stored_keys[0], key_row_block[:PREFILL_ROWS]], 0).reshape(CACHE_SLOTS_PER + PREFILL_ROWS, KEY_VALUE_HEADS, HEAD_SIZE).astype(jnp.float32)
    window_values = jnp.concatenate([stored_values[0], value_row_block[:PREFILL_ROWS]], 0).reshape(CACHE_SLOTS_PER + PREFILL_ROWS, KEY_VALUE_HEADS, HEAD_SIZE).astype(jnp.float32)
    span_scores = jnp.einsum('qhgd,khd->hgqk', window_query, window_keys) * score_scale
    key_place = jnp.arange(CACHE_SLOTS_PER + PREFILL_ROWS, dtype=jnp.int32)
    query_place = jnp.arange(PREFILL_ROWS, dtype=jnp.int32)
    allowed = jnp.where(key_place[None, :] < CACHE_SLOTS_PER, key_place[None, :] < lengths[0], key_place[None, :] - CACHE_SLOTS_PER <= query_place[:, None])
    span_scores = jnp.where(allowed, span_scores, NEG_FILL)
    span_probs = softmax_rows(span_scores).astype(jnp.float32)
    span_out = jnp.einsum('hgqk,khd->qhgd', span_probs, window_values).astype(jnp.bfloat16).reshape(PREFILL_ROWS, QUERY_HEADS * HEAD_SIZE)
    decode_query_rows = query_row_block[PREFILL_ROWS:].reshape(DECODE_REQUESTS, KEY_VALUE_HEADS, group_length, HEAD_SIZE).astype(jnp.float32)
    earlier_keys = stored_keys[1:].reshape(DECODE_REQUESTS, CACHE_SLOTS_PER, KEY_VALUE_HEADS, HEAD_SIZE).astype(jnp.float32)
    earlier_values = stored_values[1:].reshape(DECODE_REQUESTS, CACHE_SLOTS_PER, KEY_VALUE_HEADS, HEAD_SIZE).astype(jnp.float32)
    self_keys = key_row_block[PREFILL_ROWS:].reshape(DECODE_REQUESTS, KEY_VALUE_HEADS, HEAD_SIZE).astype(jnp.float32)
    self_values = value_row_block[PREFILL_ROWS:].reshape(DECODE_REQUESTS, KEY_VALUE_HEADS, HEAD_SIZE).astype(jnp.float32)
    old_scores = jnp.einsum('rhgd,rkhd->rhgk', decode_query_rows, earlier_keys) * score_scale
    in_cache = jnp.arange(CACHE_SLOTS_PER, dtype=jnp.int32)[None, :] < lengths[1:, None]
    old_scores = jnp.where(in_cache[:, None, None, :], old_scores, NEG_FILL)
    own_scores = jnp.einsum('rhgd,rhd->rhg', decode_query_rows, self_keys)[..., None] * score_scale
    decode_probs = softmax_rows(jnp.concatenate([old_scores, own_scores], -1)).astype(jnp.float32)
    decode_out = jnp.einsum('rhgk,rkhd->rhgd', decode_probs[..., :CACHE_SLOTS_PER], earlier_values)
    decode_out = decode_out + decode_probs[..., CACHE_SLOTS_PER][..., None] * self_values[:, :, None, :]
    decode_out = decode_out.astype(jnp.bfloat16).reshape(DECODE_REQUESTS, QUERY_HEADS * HEAD_SIZE)
    return jnp.concatenate([span_out, decode_out], 0)

def reference(residual, queries, fresh_rotated_keys, fresh_values, cache_keys, request_value_cache, cache_lengths, out_proj, router_weight, norm_gain, expert_ids, live_mask, w_gate, w_up, w_down):

    def one_group(group_index):
        first_row = group_index * SLOT
        first_request = group_index * (1 + DECODE_REQUESTS)
        return group_attention(lax.dynamic_slice_in_dim(queries, first_row, SLOT, 0), lax.dynamic_slice_in_dim(fresh_rotated_keys, first_row, SLOT, 0), lax.dynamic_slice_in_dim(fresh_values, first_row, SLOT, 0), lax.dynamic_slice_in_dim(cache_keys, first_request, 1 + DECODE_REQUESTS, 0), lax.dynamic_slice_in_dim(request_value_cache, first_request, 1 + DECODE_REQUESTS, 0), lax.dynamic_slice_in_dim(cache_lengths, first_request, 1 + DECODE_REQUESTS, 0))
    attended = lax.map(one_group, jnp.arange(TOKEN_ROWS // SLOT, dtype=jnp.int32)).reshape(TOKEN_ROWS, QUERY_HEADS * HEAD_SIZE)
    projected = jnp.dot(attended, out_proj, preferred_element_type=jnp.float32)
    hidden_state = (residual.astype(jnp.float32) + projected).astype(jnp.bfloat16)
    hidden32 = hidden_state.astype(jnp.float32)
    normed = (hidden32 * lax.rsqrt(lax.optimization_barrier(jnp.mean(hidden32 * hidden32, -1, keepdims=True)) + NORM_EPS) * norm_gain.astype(jnp.float32)).astype(jnp.bfloat16)
    logits = jnp.dot(normed, router_weight, preferred_element_type=jnp.float32)
    picked = jnp.take_along_axis(logits, expert_ids, 1)
    raised = jnp.exp(picked)
    gate_share = raised / lax.optimization_barrier(jnp.sum(raised, -1, keepdims=True))
    flat_ids = expert_ids.reshape(-1)
    flat_gates = gate_share.reshape(-1)
    live32 = live_mask.astype(jnp.float32)
    limit = TOKEN_ROWS // TOK_DEV * CAPE

    def one_expert(running, expert):
        matches = flat_ids == expert
        found_pairs = jnp.nonzero(matches, size=limit, fill_value=0)[0].astype(jnp.int32)
        match_count = jnp.sum(matches.astype(jnp.int32))
        in_range = jnp.arange(limit, dtype=jnp.int32) < match_count
        token_rows = found_pairs // TOPK
        inputs = normed[token_rows]
        gate_proj = jnp.dot(inputs, lax.dynamic_index_in_dim(w_gate, expert, 0, False), preferred_element_type=jnp.float32)
        up_proj = jnp.dot(inputs, lax.dynamic_index_in_dim(w_up, expert, 0, False), preferred_element_type=jnp.float32)
        activated = (jax.nn.silu(gate_proj) * up_proj).astype(jnp.bfloat16)
        outputs = jnp.dot(activated, lax.dynamic_index_in_dim(w_down, expert, 0, False), preferred_element_type=jnp.float32).astype(jnp.bfloat16)
        weighting = jnp.where(in_range, flat_gates[found_pairs] * live32[token_rows], 0.0)
        running = running.at[token_rows].add(weighting[:, None] * outputs.astype(jnp.float32))
        return (running, None)
    mixture, _ = lax.scan(one_expert, jnp.zeros((TOKEN_ROWS, D), jnp.float32), jnp.arange(EXPERTS, dtype=jnp.int32))
    return (hidden32 + mixture).astype(jnp.bfloat16)
```

```python
import math

import jax
import jax.numpy as jnp
from jax import lax
from jax.experimental import pallas as pl
from jax.experimental.pallas import tpu as pltpu
from jax.sharding import PartitionSpec as P

HEAD = 128
NEG_FILL = -1e30
NORM_EPS = 1e-06
F32 = jnp.float32
BF16 = jnp.bfloat16
VMEM = pltpu.VMEM
LIMIT = 60 * 1024 * 1024


def dot(a, b):
    return jnp.dot(a, b, preferred_element_type=F32)


def dot_nt(a, b):
    return lax.dot_general(a, b, (((1,), (1,)), ((), ())), preferred_element_type=F32)


def dot_tn(a, b):
    return lax.dot_general(a, b, (((0,), (0,)), ((), ())), preferred_element_type=F32)


def iota(shape, axis):
    return lax.broadcasted_iota(jnp.int32, shape, axis)


def softmax_parts(scores):
    top = jnp.max(scores, -1, keepdims=True)
    raised = jnp.exp(scores - top)
    return raised, jnp.sum(raised, -1, keepdims=True)


def attend_kernel(
    lens_ref, core_ref, q_ref, fk_ref, fv_ref, ck_hbm, cv_hbm, wo_hbm,
    mine_ref, other_ref,
    k_buf, v_buf, wo_buf, att, acc, dq, dk, dv, ds, do, sem,
):
    rows, width = q_ref.shape
    requests, slots, kvw = k_buf.shape
    decode = requests - 1
    span = rows - decode
    kvh = kvw // HEAD
    heads = width // HEAD
    per = heads // kvh
    scale = 1.0 / math.sqrt(HEAD)
    half = requests // 2 + 1

    cuts = ((0, 1), (1, half), (half, requests))
    copies = []
    for i, (lo, hi) in enumerate(cuts):
        copies.append(pltpu.make_async_copy(ck_hbm.at[pl.ds(lo, hi - lo)], k_buf.at[pl.ds(lo, hi - lo)], sem.at[0, i]))
        copies.append(pltpu.make_async_copy(cv_hbm.at[pl.ds(lo, hi - lo)], v_buf.at[pl.ds(lo, hi - lo)], sem.at[1, i]))
    pieces = 4
    step = wo_buf.shape[0] // pieces
    weights = [
        pltpu.make_async_copy(wo_hbm.at[pl.ds(i * step, step)], wo_buf.at[pl.ds(i * step, step)], sem.at[2, i])
        for i in range(pieces)
    ]
    for c in copies + weights:
        c.start()

    tail = q_ref[span:, :].astype(F32)
    tail_k = fk_ref[span:, :].astype(F32)
    tail_v = fv_ref[span:, :].astype(F32)
    for h in range(heads):
        g = h // per
        dq[pl.ds(h, decode, stride=heads), :] = tail[:, h * HEAD : (h + 1) * HEAD]
        dk[pl.ds(h, decode, stride=heads), :] = tail_k[:, g * HEAD : (g + 1) * HEAD]
        dv[pl.ds(h, decode, stride=heads), :] = tail_v[:, g * HEAD : (g + 1) * HEAD]

    copies[0].wait()
    copies[1].wait()
    total = slots + span
    shape = (per * span, total)
    col = iota(shape, 1)
    place = iota(shape, 0) & (span - 1)
    allowed = ((col < slots) & (col < lens_ref[0])) | ((col >= slots) & (col - slots <= place))
    for g in range(kvh):
        gs = slice(g * HEAD, (g + 1) * HEAD)
        q = jnp.concatenate(
            [q_ref[:span, (g * per + j) * HEAD : (g * per + j + 1) * HEAD] for j in range(per)], 0
        )
        k = jnp.concatenate([k_buf[0, :, gs], fk_ref[:span, gs]], 0)
        v = jnp.concatenate([v_buf[0, :, gs], fv_ref[:span, gs]], 0)
        s = jnp.where(allowed, dot_nt(q, k) * scale, NEG_FILL)
        raised, norm = softmax_parts(s)
        p = (raised * (1.0 / norm)).astype(BF16)
        o = dot(p, v).astype(BF16)
        for j in range(per):
            h = g * per + j
            att[:span, h * HEAD : (h + 1) * HEAD] = o[j * span : (j + 1) * span]

    pairs = decode * heads
    lower = (iota((pairs, HEAD), 0) & (heads - 1)) < per
    qv = dq[...]
    qbd = jnp.concatenate([jnp.where(lower, qv, 0.0), jnp.where(lower, 0.0, qv)], 1).astype(BF16)
    own = jnp.sum(qv * dk[...], -1, keepdims=True) * scale
    lane = iota((heads, slots), 1)
    for r in range(decode):
        if r == 0:
            copies[2].wait()
        if r + 1 == half:
            copies[4].wait()
        s = dot_nt(qbd[r * heads : (r + 1) * heads], k_buf[r + 1]) * scale
        ds[r * heads : (r + 1) * heads, :] = jnp.where(lane < lens_ref[r + 1], s, NEG_FILL)
    s = ds[...]
    top = jnp.maximum(jnp.max(s, -1, keepdims=True), own)
    raised = jnp.exp(s - top)
    own_raised = jnp.exp(own - top)
    inv = 1.0 / (jnp.sum(raised, -1, keepdims=True) + own_raised)
    p = (raised * inv).astype(BF16)
    own_p = (own_raised * inv).astype(BF16).astype(F32)
    copies[3].wait()
    copies[5].wait()
    for r in range(decode):
        o = dot(p[r * heads : (r + 1) * heads], v_buf[r + 1])
        do[r * heads : r * heads + per, :] = o[:per, :HEAD]
        do[r * heads + per : (r + 1) * heads, :] = o[per:, HEAD:]
    do[...] = do[...] + own_p * dv[...]
    for h in range(heads):
        att[span:, h * HEAD : (h + 1) * HEAD] = do[pl.ds(h, decode, stride=heads), :].astype(BF16)

    for i in range(pieces):
        weights[i].wait()
    cols = wo_buf.shape[1]
    block = cols // 4
    a = att[...]
    for n in range(4):
        acc[:, n * block : (n + 1) * block] = dot(a, wo_buf[:, n * block : (n + 1) * block])
    own_rows = mine_ref.shape[0]
    core = core_ref[0]
    first = pl.multiple_of(core * own_rows, 8)
    second = pl.multiple_of((1 - core) * own_rows, 8)
    mine_ref[...] = acc[pl.ds(first, own_rows), :]
    other_ref[...] = acc[pl.ds(second, own_rows), :]


def attend(lens, core, q, fk, fv, ck, cv, wo):
    rows, width = q.shape
    requests, slots, kvw = ck.shape
    heads = width // HEAD
    pairs = (requests - 1) * heads
    own = rows // 2
    vm = pl.BlockSpec(memory_space=VMEM)
    sm = pl.BlockSpec(memory_space=pltpu.SMEM)
    hb = pl.BlockSpec(memory_space=pl.ANY)
    out = jax.ShapeDtypeStruct((own, wo.shape[1]), F32)
    return pl.pallas_call(
        attend_kernel,
        name="attend",
        out_shape=(out, out),
        in_specs=[sm, sm, vm, vm, vm, hb, hb, hb],
        out_specs=(vm, vm),
        scratch_shapes=[
            VMEM(ck.shape, BF16),
            VMEM(cv.shape, BF16),
            VMEM(wo.shape, BF16),
            VMEM((rows, width), BF16),
            VMEM((rows, wo.shape[1]), F32),
            VMEM((pairs, HEAD), F32),
            VMEM((pairs, HEAD), F32),
            VMEM((pairs, HEAD), F32),
            VMEM((pairs, slots), F32),
            VMEM((pairs, HEAD), F32),
            pltpu.SemaphoreType.DMA((3, 4)),
        ],
        compiler_params=pltpu.CompilerParams(vmem_limit_bytes=LIMIT),
    )(lens, core, q, fk, fv, ck, cv, wo)


MAIN = 8


def spread_last(scr, rows):
    tiles = scr.shape[0]
    for q in range(MAIN):
        for j in range(tiles):
            at = (q * tiles + j) * HEAD
            scr[j, pl.ds(q, rows.shape[0], stride=MAIN), :] = rows[:, at : at + HEAD]
    return jnp.concatenate([scr[j] for j in range(tiles)], 1).astype(BF16)


def collect_last(scr, pieces, count):
    tiles = scr.shape[0]
    pieces = pieces.astype(F32)
    for j in range(tiles):
        scr[j] = pieces[:, j * HEAD : (j + 1) * HEAD]
    rows = [scr[j, pl.ds(q, count, stride=MAIN), :] for q in range(MAIN) for j in range(tiles)]
    return jnp.concatenate(rows, 1).astype(BF16)


def last_scratch(rows, width):
    return VMEM((width // MAIN // HEAD, rows, HEAD), F32)


def expander(experts):
    shape = (experts, experts * MAIN)
    return ((iota(shape, 1) >> 3) == iota(shape, 0)).astype(F32).astype(BF16)


def route_kernel(
    res_ref, mine_ref, recv_ref, router_ref, gain_ref, ids_ref, live_ref,
    hidden_ref, gate_ref, rank_ref, send_ref, scr,
):
    rows, width = res_ref.shape
    experts = router_ref.shape[1]
    hidden = (res_ref[...].astype(F32) + (mine_ref[...] + recv_ref[...])).astype(BF16)
    hidden_ref[...] = hidden
    h32 = hidden.astype(F32)
    mean = jnp.mean(h32 * h32, -1, keepdims=True)
    normed = (h32 * lax.rsqrt(mean + NORM_EPS) * gain_ref[...].astype(F32)).astype(BF16)
    logits = dot(normed, router_ref[...])
    lane = iota((rows, experts), 1)
    ids = ids_ref[...]
    chosen = ids[:, 0:1] == lane
    for k in range(1, ids.shape[1]):
        chosen = chosen | (ids[:, k : k + 1] == lane)
    raised = jnp.where(chosen, jnp.exp(jnp.where(chosen, logits, 0.0)), 0.0)
    gate_ref[...] = raised / jnp.sum(raised, -1, keepdims=True)
    used = jnp.where(chosen & (live_ref[...] > 0), 1.0, 0.0)
    before = (iota((rows, rows), 0) > iota((rows, rows), 1)).astype(F32).astype(BF16)
    rank = used * (dot(before, used.astype(BF16)) + 1.0)
    rank_ref[...] = rank
    spread = dot(rank.astype(BF16), expander(experts))
    slot = (iota(spread.shape, 1) & (MAIN - 1)).astype(F32) + 1.0
    pick = jnp.where(spread == slot, 1.0, 0.0).astype(BF16)
    block = width // 4
    for n in range(4):
        cs = slice(n * block, (n + 1) * block)
        send_ref[:, cs] = dot_tn(pick, normed[:, cs]).astype(BF16)
    last = jnp.where(rank == MAIN + 1.0, 1.0, 0.0).astype(BF16)
    send_ref[:, width:] = spread_last(scr, dot_tn(last, normed))


def route(res, mine, recv, router, gain, ids, live):
    rows, width = res.shape
    experts = router.shape[1]
    part = width // MAIN
    vm = pl.BlockSpec(memory_space=VMEM)
    return pl.pallas_call(
        route_kernel,
        name="route",
        out_shape=(
            jax.ShapeDtypeStruct((rows, width), BF16),
            jax.ShapeDtypeStruct((rows, experts), F32),
            jax.ShapeDtypeStruct((rows, experts), F32),
            jax.ShapeDtypeStruct((experts * MAIN, width + part), BF16),
        ),
        in_specs=[vm] * 7,
        out_specs=(vm,) * 4,
        scratch_shapes=[last_scratch(experts * MAIN, width)],
        compiler_params=pltpu.CompilerParams(vmem_limit_bytes=LIMIT),
    )(res, mine, recv, router, gain, ids, live)


def expert_kernel(x_ref, wg_hbm, wu_hbm, wd_hbm, y_ref, wg, wu, wd, scr, sem):
    width = wg.shape[0]
    copies = [
        pltpu.make_async_copy(wg_hbm.at[0], wg, sem.at[0]),
        pltpu.make_async_copy(wu_hbm.at[0], wu, sem.at[1]),
        pltpu.make_async_copy(wd_hbm.at[0], wd, sem.at[2]),
    ]
    for c in copies:
        c.start()

    def mlp(x):
        g = dot(x, wg[...])
        u = dot(x, wu[...])
        return dot((g * jax.nn.sigmoid(g) * u).astype(BF16), wd[...])

    count = x_ref.shape[0]
    last = collect_last(scr, x_ref[:, width:], count // MAIN)
    for c in copies:
        c.wait()
    y_ref[:, width:] = spread_last(scr, mlp(last))
    chunk = 256

    @pl.loop(0, count // chunk)
    def _(i):
        rows = pl.ds(pl.multiple_of(i * chunk, chunk), chunk)
        y_ref[rows, :width] = mlp(x_ref[rows, :width]).astype(BF16)


def expert(x, wg, wu, wd):
    vm = pl.BlockSpec(memory_space=VMEM)
    hb = pl.BlockSpec(memory_space=pl.ANY)
    return pl.pallas_call(
        expert_kernel,
        name="expert",
        out_shape=jax.ShapeDtypeStruct(x.shape, BF16),
        in_specs=[vm, hb, hb, hb],
        out_specs=vm,
        scratch_shapes=[
            VMEM(wg.shape[1:], BF16),
            VMEM(wu.shape[1:], BF16),
            VMEM(wd.shape[1:], BF16),
            last_scratch(x.shape[0], wg.shape[1]),
            pltpu.SemaphoreType.DMA((3,)),
        ],
        compiler_params=pltpu.CompilerParams(vmem_limit_bytes=LIMIT),
    )(x, wg, wu, wd)


def combine_kernel(hidden_ref, gate_ref, rank_ref, y_ref, out_ref, scr):
    rows, width = hidden_ref.shape
    experts = gate_ref.shape[1]
    rank = rank_ref[...]
    gate = gate_ref[...]
    high = gate.astype(BF16).astype(F32)
    both = jnp.concatenate([high, gate - high], 0)
    rank2 = jnp.concatenate([rank, rank], 0)
    grow = expander(experts)
    spread = dot(rank2.astype(BF16), grow)
    slot = (iota(spread.shape, 1) & (MAIN - 1)).astype(F32) + 1.0
    main = jnp.where(spread == slot, dot(both.astype(BF16), grow), 0.0).astype(BF16)
    last = jnp.where(rank2 == MAIN + 1.0, both, 0.0).astype(BF16)
    tail = collect_last(scr, y_ref[:, width:], experts)
    block = width // 4
    for n in range(4):
        cs = slice(n * block, (n + 1) * block)
        mix = dot(main, y_ref[:, cs]) + dot(last, tail[:, cs])
        out_ref[:, cs] = (hidden_ref[:, cs].astype(F32) + (mix[:rows] + mix[rows:])).astype(BF16)


def combine(hidden, gate, rank, y):
    vm = pl.BlockSpec(memory_space=VMEM)
    return pl.pallas_call(
        combine_kernel,
        name="combine",
        out_shape=jax.ShapeDtypeStruct(hidden.shape, BF16),
        in_specs=[vm] * 4,
        out_specs=vm,
        scratch_shapes=[last_scratch(y.shape[0], hidden.shape[1])],
        compiler_params=pltpu.CompilerParams(vmem_limit_bytes=LIMIT),
    )(hidden, gate, rank, y)


def exchange(x, experts):
    blocks = x.reshape(experts, MAIN, x.shape[1])
    moved = lax.all_to_all(blocks, ("ep", "dp"), split_axis=0, concat_axis=0, tiled=True)
    return moved.reshape(x.shape)


def on_device(
    residual, queries, fresh_rotated_keys, fresh_values, cache_keys, request_value_cache,
    cache_lengths, out_proj, router_weight, norm_gain, expert_ids, live_mask,
    w_gate, w_up, w_down,
):
    experts = router_weight.shape[1]
    core = lax.axis_index("dp").astype(jnp.int32).reshape(1)
    mine, other = attend(
        cache_lengths, core, queries, fresh_rotated_keys, fresh_values, cache_keys,
        request_value_cache, out_proj,
    )
    recv = lax.ppermute(other, "dp", [(0, 1), (1, 0)])
    hidden, gate, rank, send = route(
        residual, mine, recv, router_weight, norm_gain.reshape(1, -1), expert_ids,
        live_mask.reshape(-1, 1),
    )
    back = exchange(expert(exchange(send, experts), w_gate, w_up, w_down), experts)
    return combine(hidden, gate, rank, back)


def solution(mesh):
    both = ("ep", "dp")
    placed = (
        P(both, None),
        P("ep", "dp"),
        P("ep", "dp"),
        P("ep", "dp"),
        P("ep", None, "dp"),
        P("ep", None, "dp"),
        P("ep"),
        P("dp", None),
        P(),
        P(),
        P(both, None),
        P(both),
        P(both, None, None),
        P(both, None, None),
        P(both, None, None),
    )
    return jax.shard_map(
        on_device, mesh=mesh, in_specs=placed, out_specs=P(both, None), check_vma=False
    )
```

```python
import math

import jax
import jax.numpy as jnp
from jax import lax
from jax.experimental import pallas as pl
from jax.experimental.pallas import tpu as pltpu
from jax.sharding import PartitionSpec as P

HEAD = 128
NEG_FILL = -1e30
NORM_EPS = 1e-06
F32 = jnp.float32
BF16 = jnp.bfloat16
VMEM = pltpu.VMEM
LIMIT = 30 * 1024 * 1024
FULL = 60 * 1024 * 1024


def dot(a, b):
    return jnp.dot(a, b, preferred_element_type=F32)


def dot_nt(a, b):
    return lax.dot_general(a, b, (((1,), (1,)), ((), ())), preferred_element_type=F32)


def dot_tn(a, b):
    return lax.dot_general(a, b, (((0,), (0,)), ((), ())), preferred_element_type=F32)


def iota(shape, axis):
    return lax.broadcasted_iota(jnp.int32, shape, axis)


def softmax_parts(scores):
    top = jnp.max(scores, -1, keepdims=True)
    raised = jnp.exp(scores - top)
    return raised, jnp.sum(raised, -1, keepdims=True)


def attend_kernel(
    lens_ref, core_ref, q_hbm, fk_hbm, fv_hbm, ck_hbm, cv_hbm, wo_hbm,
    mine_ref, other_ref,
    q_ref, fk_ref, fv_ref, k_buf, v_buf, wo_buf, att, acc, dq, dk, dv, ds, do, sem,
):
    rows, width = q_ref.shape
    requests, slots, kvw = k_buf.shape
    decode = requests - 1
    span = rows - decode
    kvh = kvw // HEAD
    heads = width // HEAD
    per = heads // kvh
    scale = 1.0 / math.sqrt(HEAD)
    half = requests // 2 + 1

    cuts = ((0, 1), (1, half), (half, requests))
    copies = []
    for i, (lo, hi) in enumerate(cuts):
        copies.append(pltpu.make_async_copy(ck_hbm.at[pl.ds(lo, hi - lo)], k_buf.at[pl.ds(lo, hi - lo)], sem.at[0, i]))
        copies.append(pltpu.make_async_copy(cv_hbm.at[pl.ds(lo, hi - lo)], v_buf.at[pl.ds(lo, hi - lo)], sem.at[1, i]))
    pieces = 4
    step = wo_buf.shape[0] // pieces
    weights = [
        pltpu.make_async_copy(wo_hbm.at[pl.ds(i * step, step)], wo_buf.at[pl.ds(i * step, step)], sem.at[2, i])
        for i in range(pieces)
    ]
    small = [
        pltpu.make_async_copy(src, dst, sem.at[3, i])
        for i, (src, dst) in enumerate(((q_hbm, q_ref), (fk_hbm, fk_ref), (fv_hbm, fv_ref)))
    ]
    for c in small + copies + weights:
        c.start()
    for c in small:
        c.wait()

    tail = q_ref[span:, :].astype(F32)
    tail_k = fk_ref[span:, :].astype(F32)
    tail_v = fv_ref[span:, :].astype(F32)
    for h in range(heads):
        g = h // per
        dq[pl.ds(h, decode, stride=heads), :] = tail[:, h * HEAD : (h + 1) * HEAD]
        dk[pl.ds(h, decode, stride=heads), :] = tail_k[:, g * HEAD : (g + 1) * HEAD]
        dv[pl.ds(h, decode, stride=heads), :] = tail_v[:, g * HEAD : (g + 1) * HEAD]

    copies[0].wait()
    copies[1].wait()
    total = slots + span
    shape = (per * span, total)
    col = iota(shape, 1)
    place = iota(shape, 0) & (span - 1)
    allowed = ((col < slots) & (col < lens_ref[0])) | ((col >= slots) & (col - slots <= place))
    for g in range(kvh):
        gs = slice(g * HEAD, (g + 1) * HEAD)
        q = jnp.concatenate(
            [q_ref[:span, (g * per + j) * HEAD : (g * per + j + 1) * HEAD] for j in range(per)], 0
        )
        k = jnp.concatenate([k_buf[0, :, gs], fk_ref[:span, gs]], 0)
        v = jnp.concatenate([v_buf[0, :, gs], fv_ref[:span, gs]], 0)
        s = jnp.where(allowed, dot_nt(q, k) * scale, NEG_FILL)
        raised, norm = softmax_parts(s)
        p = (raised * (1.0 / norm)).astype(BF16)
        o = dot(p, v).astype(BF16)
        for j in range(per):
            h = g * per + j
            att[:span, h * HEAD : (h + 1) * HEAD] = o[j * span : (j + 1) * span]

    pairs = decode * heads
    lower = (iota((pairs, HEAD), 0) & (heads - 1)) < per
    qv = dq[...]
    qbd = jnp.concatenate([jnp.where(lower, qv, 0.0), jnp.where(lower, 0.0, qv)], 1).astype(BF16)
    own = jnp.sum(qv * dk[...], -1, keepdims=True) * scale
    lane = iota((heads, slots), 1)
    for r in range(decode):
        if r == 0:
            copies[2].wait()
        if r + 1 == half:
            copies[4].wait()
        s = dot_nt(qbd[r * heads : (r + 1) * heads], k_buf[r + 1]) * scale
        ds[r * heads : (r + 1) * heads, :] = jnp.where(lane < lens_ref[r + 1], s, NEG_FILL)
    s = ds[...]
    top = jnp.maximum(jnp.max(s, -1, keepdims=True), own)
    raised = jnp.exp(s - top)
    own_raised = jnp.exp(own - top)
    inv = 1.0 / (jnp.sum(raised, -1, keepdims=True) + own_raised)
    p = (raised * inv).astype(BF16)
    own_p = (own_raised * inv).astype(BF16).astype(F32)
    copies[3].wait()
    copies[5].wait()
    for r in range(decode):
        o = dot(p[r * heads : (r + 1) * heads], v_buf[r + 1])
        do[r * heads : r * heads + per, :] = o[:per, :HEAD]
        do[r * heads + per : (r + 1) * heads, :] = o[per:, HEAD:]
    do[...] = do[...] + own_p * dv[...]
    for h in range(heads):
        att[span:, h * HEAD : (h + 1) * HEAD] = do[pl.ds(h, decode, stride=heads), :].astype(BF16)

    for i in range(pieces):
        weights[i].wait()
    cols = wo_buf.shape[1]
    block = cols // 4
    a = att[...]
    for n in range(4):
        acc[:, n * block : (n + 1) * block] = dot(a, wo_buf[:, n * block : (n + 1) * block])
    own_rows = mine_ref.shape[0]
    core = core_ref[0]
    first = pl.multiple_of(core * own_rows, 8)
    second = pl.multiple_of((1 - core) * own_rows, 8)
    mine_ref[...] = acc[pl.ds(first, own_rows), :]
    other_ref[...] = acc[pl.ds(second, own_rows), :]


def attend(lens, core, q, fk, fv, ck, cv, wo):
    rows, width = q.shape
    requests, slots, kvw = ck.shape
    heads = width // HEAD
    pairs = (requests - 1) * heads
    own = rows // 2
    vm = pl.BlockSpec(memory_space=VMEM)
    sm = pl.BlockSpec(memory_space=pltpu.SMEM)
    hb = pl.BlockSpec(memory_space=pl.ANY)
    out = jax.ShapeDtypeStruct((own, wo.shape[1]), F32)
    return pl.pallas_call(
        attend_kernel,
        name="attend",
        out_shape=(out, out),
        in_specs=[sm, sm] + [hb] * 6,
        out_specs=(vm, vm),
        scratch_shapes=[
            VMEM(q.shape, BF16),
            VMEM(fk.shape, BF16),
            VMEM(fv.shape, BF16),
            VMEM(ck.shape, BF16),
            VMEM(cv.shape, BF16),
            VMEM(wo.shape, BF16),
            VMEM((rows, width), BF16),
            VMEM((rows, wo.shape[1]), F32),
            VMEM((pairs, HEAD), F32),
            VMEM((pairs, HEAD), F32),
            VMEM((pairs, HEAD), F32),
            VMEM((pairs, slots), F32),
            VMEM((pairs, HEAD), F32),
            pltpu.SemaphoreType.DMA((4, 4)),
        ],
        compiler_params=pltpu.CompilerParams(vmem_limit_bytes=FULL),
    )(lens, core, q, fk, fv, ck, cv, wo)


MAIN = 8


def spread_last(scr, rows):
    tiles = scr.shape[0]
    for q in range(MAIN):
        for j in range(tiles):
            at = (q * tiles + j) * HEAD
            scr[j, pl.ds(q, rows.shape[0], stride=MAIN), :] = rows[:, at : at + HEAD]
    return jnp.concatenate([scr[j] for j in range(tiles)], 1).astype(BF16)


def collect_last(scr, pieces, count):
    tiles = scr.shape[0]
    pieces = pieces.astype(F32)
    for j in range(tiles):
        scr[j] = pieces[:, j * HEAD : (j + 1) * HEAD]
    rows = [scr[j, pl.ds(q, count, stride=MAIN), :] for q in range(MAIN) for j in range(tiles)]
    return jnp.concatenate(rows, 1).astype(BF16)


def last_scratch(rows, width):
    return VMEM((width // MAIN // HEAD, rows, HEAD), F32)


def expander(experts):
    shape = (experts, experts * MAIN)
    return ((iota(shape, 1) >> 3) == iota(shape, 0)).astype(F32).astype(BF16)


def route_kernel(
    res_ref, mine_ref, recv_ref, router_ref, gain_ref, ids_ref, live_ref,
    hidden_ref, gate_ref, rank_ref, send_ref, scr,
):
    rows, width = res_ref.shape
    experts = router_ref.shape[1]
    hidden = (res_ref[...].astype(F32) + (mine_ref[...] + recv_ref[...])).astype(BF16)
    hidden_ref[...] = hidden
    h32 = hidden.astype(F32)
    mean = jnp.mean(h32 * h32, -1, keepdims=True)
    normed = (h32 * lax.rsqrt(mean + NORM_EPS) * gain_ref[...].astype(F32)).astype(BF16)
    logits = dot(normed, router_ref[...])
    lane = iota((rows, experts), 1)
    ids = ids_ref[...]
    chosen = ids[:, 0:1] == lane
    for k in range(1, ids.shape[1]):
        chosen = chosen | (ids[:, k : k + 1] == lane)
    raised = jnp.where(chosen, jnp.exp(jnp.where(chosen, logits, 0.0)), 0.0)
    gate_ref[...] = raised / jnp.sum(raised, -1, keepdims=True)
    used = jnp.where(chosen & (live_ref[...] > 0), 1.0, 0.0)
    before = (iota((rows, rows), 0) > iota((rows, rows), 1)).astype(F32).astype(BF16)
    rank = used * (dot(before, used.astype(BF16)) + 1.0)
    rank_ref[...] = rank
    spread = dot(rank.astype(BF16), expander(experts))
    slot = (iota(spread.shape, 1) & (MAIN - 1)).astype(F32) + 1.0
    pick = jnp.where(spread == slot, 1.0, 0.0).astype(BF16)
    block = width // 4
    for n in range(4):
        cs = slice(n * block, (n + 1) * block)
        send_ref[:, cs] = dot_tn(pick, normed[:, cs]).astype(BF16)
    last = jnp.where(rank == MAIN + 1.0, 1.0, 0.0).astype(BF16)
    send_ref[:, width:] = spread_last(scr, dot_tn(last, normed))


def route(res, mine, recv, router, gain, ids, live):
    rows, width = res.shape
    experts = router.shape[1]
    part = width // MAIN
    vm = pl.BlockSpec(memory_space=VMEM)
    return pl.pallas_call(
        route_kernel,
        name="route",
        out_shape=(
            jax.ShapeDtypeStruct((rows, width), BF16),
            jax.ShapeDtypeStruct((rows, experts), F32),
            jax.ShapeDtypeStruct((rows, experts), F32),
            jax.ShapeDtypeStruct((experts * MAIN, width + part), BF16),
        ),
        in_specs=[vm] * 7,
        out_specs=(vm,) * 4,
        scratch_shapes=[last_scratch(experts * MAIN, width)],
        compiler_params=pltpu.CompilerParams(vmem_limit_bytes=LIMIT),
    )(res, mine, recv, router, gain, ids, live)


def expert_kernel(x_ref, wg_ref, wu_ref, wd_ref, y_ref, scr):
    wg, wu, wd = wg_ref.at[0], wu_ref.at[0], wd_ref.at[0]
    width = wg.shape[0]

    def mlp(x):
        g = dot(x, wg[...])
        u = dot(x, wu[...])
        return dot((g * jax.nn.sigmoid(g) * u).astype(BF16), wd[...])

    count = x_ref.shape[0]
    last = collect_last(scr, x_ref[:, width:], count // MAIN)
    y_ref[:, width:] = spread_last(scr, mlp(last))
    chunk = 256

    @pl.loop(0, count // chunk)
    def _(i):
        rows = pl.ds(pl.multiple_of(i * chunk, chunk), chunk)
        y_ref[rows, :width] = mlp(x_ref[rows, :width]).astype(BF16)


def expert(x, wg, wu, wd):
    vm = pl.BlockSpec(memory_space=VMEM)
    return pl.pallas_call(
        expert_kernel,
        name="expert",
        out_shape=jax.ShapeDtypeStruct(x.shape, BF16),
        in_specs=[vm] * 4,
        out_specs=vm,
        scratch_shapes=[last_scratch(x.shape[0], wg.shape[1])],
        compiler_params=pltpu.CompilerParams(vmem_limit_bytes=LIMIT),
    )(x, wg, wu, wd)


def combine_kernel(hidden_ref, gate_ref, rank_ref, y_ref, out_ref, scr):
    rows, width = hidden_ref.shape
    experts = gate_ref.shape[1]
    rank = rank_ref[...]
    gate = gate_ref[...]
    high = gate.astype(BF16).astype(F32)
    both = jnp.concatenate([high, gate - high], 0)
    rank2 = jnp.concatenate([rank, rank], 0)
    grow = expander(experts)
    spread = dot(rank2.astype(BF16), grow)
    slot = (iota(spread.shape, 1) & (MAIN - 1)).astype(F32) + 1.0
    main = jnp.where(spread == slot, dot(both.astype(BF16), grow), 0.0).astype(BF16)
    last = jnp.where(rank2 == MAIN + 1.0, both, 0.0).astype(BF16)
    tail = collect_last(scr, y_ref[:, width:], experts)
    block = width // 4
    for n in range(4):
        cs = slice(n * block, (n + 1) * block)
        mix = dot(main, y_ref[:, cs]) + dot(last, tail[:, cs])
        out_ref[:, cs] = (hidden_ref[:, cs].astype(F32) + (mix[:rows] + mix[rows:])).astype(BF16)


def combine(hidden, gate, rank, y):
    vm = pl.BlockSpec(memory_space=VMEM)
    return pl.pallas_call(
        combine_kernel,
        name="combine",
        out_shape=jax.ShapeDtypeStruct(hidden.shape, BF16),
        in_specs=[vm] * 4,
        out_specs=vm,
        scratch_shapes=[last_scratch(y.shape[0], hidden.shape[1])],
        compiler_params=pltpu.CompilerParams(vmem_limit_bytes=LIMIT),
    )(hidden, gate, rank, y)


def exchange(x, experts):
    blocks = x.reshape(experts, MAIN, x.shape[1])
    moved = lax.all_to_all(blocks, ("ep", "dp"), split_axis=0, concat_axis=0, tiled=True)
    return moved.reshape(x.shape)


def on_device(
    residual, queries, fresh_rotated_keys, fresh_values, cache_keys, request_value_cache,
    cache_lengths, out_proj, router_weight, norm_gain, expert_ids, live_mask,
    w_gate, w_up, w_down,
):
    experts = router_weight.shape[1]
    core = lax.axis_index("dp").astype(jnp.int32).reshape(1)
    mine, other = attend(
        cache_lengths, core, queries, fresh_rotated_keys, fresh_values, cache_keys,
        request_value_cache, out_proj,
    )
    recv = lax.ppermute(other, "dp", [(0, 1), (1, 0)])
    hidden, gate, rank, send = route(
        residual, mine, recv, router_weight, norm_gain.reshape(1, -1), expert_ids,
        live_mask.reshape(-1, 1),
    )
    back = exchange(expert(exchange(send, experts), w_gate, w_up, w_down), experts)
    return combine(hidden, gate, rank, back)


def solution(mesh):
    both = ("ep", "dp")
    placed = (
        P(both, None),
        P("ep", "dp"),
        P("ep", "dp"),
        P("ep", "dp"),
        P("ep", None, "dp"),
        P("ep", None, "dp"),
        P("ep"),
        P("dp", None),
        P(),
        P(),
        P(both, None),
        P(both),
        P(both, None, None),
        P(both, None, None),
        P(both, None, None),
    )
    return jax.shard_map(
        on_device, mesh=mesh, in_specs=placed, out_specs=P(both, None), check_vma=False
    )
```

```python
import math

import jax
import jax.numpy as jnp
from jax import lax
from jax.experimental import pallas as pl
from jax.experimental.pallas import tpu as pltpu
from jax.sharding import PartitionSpec as P

HEAD = 128
NEG_FILL = -1e30
NORM_EPS = 1e-06
F32 = jnp.float32
BF16 = jnp.bfloat16
VMEM = pltpu.VMEM
LIMIT = 30 * 1024 * 1024
FULL = 60 * 1024 * 1024


def dot(a, b):
    return jnp.dot(a, b, preferred_element_type=F32)


def dot_nt(a, b):
    return lax.dot_general(a, b, (((1,), (1,)), ((), ())), preferred_element_type=F32)


def dot_tn(a, b):
    return lax.dot_general(a, b, (((0,), (0,)), ((), ())), preferred_element_type=F32)


def iota(shape, axis):
    return lax.broadcasted_iota(jnp.int32, shape, axis)


def softmax_parts(scores):
    top = jnp.max(scores, -1, keepdims=True)
    raised = jnp.exp(scores - top)
    return raised, jnp.sum(raised, -1, keepdims=True)


def attend_kernel(
    lens_ref, core_ref, q_hbm, fk_hbm, fv_hbm, ck_hbm, cv_hbm, wo_hbm,
    mine_hbm, other_hbm,
    q_ref, fk_ref, fv_ref, k_buf, v_buf, wo_buf, att, acc, dq, dk, dv, ds, do, sem,
):
    rows, width = q_ref.shape
    requests, slots, kvw = k_buf.shape
    decode = requests - 1
    span = rows - decode
    kvh = kvw // HEAD
    heads = width // HEAD
    per = heads // kvh
    scale = 1.0 / math.sqrt(HEAD)
    half = requests // 2 + 1

    cuts = ((0, 1), (1, half), (half, requests))
    copies = []
    for i, (lo, hi) in enumerate(cuts):
        copies.append(pltpu.make_async_copy(ck_hbm.at[pl.ds(lo, hi - lo)], k_buf.at[pl.ds(lo, hi - lo)], sem.at[0, i]))
        copies.append(pltpu.make_async_copy(cv_hbm.at[pl.ds(lo, hi - lo)], v_buf.at[pl.ds(lo, hi - lo)], sem.at[1, i]))
    pieces = 4
    step = wo_buf.shape[1] // pieces
    weights = [
        pltpu.make_async_copy(wo_hbm.at[:, pl.ds(i * step, step)], wo_buf.at[:, pl.ds(i * step, step)], sem.at[2, i])
        for i in range(pieces)
    ]
    small = [
        pltpu.make_async_copy(src, dst, sem.at[3, i])
        for i, (src, dst) in enumerate(((q_hbm, q_ref), (fk_hbm, fk_ref), (fv_hbm, fv_ref)))
    ]
    for c in small + copies + weights:
        c.start()
    for c in small:
        c.wait()

    tail = q_ref[span:, :].astype(F32)
    tail_k = fk_ref[span:, :].astype(F32)
    tail_v = fv_ref[span:, :].astype(F32)
    for h in range(heads):
        g = h // per
        dq[pl.ds(h, decode, stride=heads), :] = tail[:, h * HEAD : (h + 1) * HEAD]
        dk[pl.ds(h, decode, stride=heads), :] = tail_k[:, g * HEAD : (g + 1) * HEAD]
        dv[pl.ds(h, decode, stride=heads), :] = tail_v[:, g * HEAD : (g + 1) * HEAD]

    copies[0].wait()
    copies[1].wait()
    total = slots + span
    shape = (per * span, total)
    col = iota(shape, 1)
    place = iota(shape, 0) & (span - 1)
    allowed = ((col < slots) & (col < lens_ref[0])) | ((col >= slots) & (col - slots <= place))
    for g in range(kvh):
        gs = slice(g * HEAD, (g + 1) * HEAD)
        q = jnp.concatenate(
            [q_ref[:span, (g * per + j) * HEAD : (g * per + j + 1) * HEAD] for j in range(per)], 0
        )
        k = jnp.concatenate([k_buf[0, :, gs], fk_ref[:span, gs]], 0)
        v = jnp.concatenate([v_buf[0, :, gs], fv_ref[:span, gs]], 0)
        s = jnp.where(allowed, dot_nt(q, k) * scale, NEG_FILL)
        raised, norm = softmax_parts(s)
        p = (raised * (1.0 / norm)).astype(BF16)
        o = dot(p, v).astype(BF16)
        for j in range(per):
            h = g * per + j
            att[:span, h * HEAD : (h + 1) * HEAD] = o[j * span : (j + 1) * span]

    pairs = decode * heads
    lower = (iota((pairs, HEAD), 0) & (heads - 1)) < per
    qv = dq[...]
    qbd = jnp.concatenate([jnp.where(lower, qv, 0.0), jnp.where(lower, 0.0, qv)], 1).astype(BF16)
    own = jnp.sum(qv * dk[...], -1, keepdims=True) * scale
    lane = iota((heads, slots), 1)
    for r in range(decode):
        if r == 0:
            copies[2].wait()
        if r + 1 == half:
            copies[4].wait()
        s = dot_nt(qbd[r * heads : (r + 1) * heads], k_buf[r + 1]) * scale
        ds[r * heads : (r + 1) * heads, :] = jnp.where(lane < lens_ref[r + 1], s, NEG_FILL)
    s = ds[...]
    top = jnp.maximum(jnp.max(s, -1, keepdims=True), own)
    raised = jnp.exp(s - top)
    own_raised = jnp.exp(own - top)
    inv = 1.0 / (jnp.sum(raised, -1, keepdims=True) + own_raised)
    p = (raised * inv).astype(BF16)
    own_p = (own_raised * inv).astype(BF16).astype(F32)
    copies[3].wait()
    copies[5].wait()
    for r in range(decode):
        o = dot(p[r * heads : (r + 1) * heads], v_buf[r + 1])
        do[r * heads : r * heads + per, :] = o[:per, :HEAD]
        do[r * heads + per : (r + 1) * heads, :] = o[per:, HEAD:]
    do[...] = do[...] + own_p * dv[...]
    for h in range(heads):
        att[span:, h * HEAD : (h + 1) * HEAD] = do[pl.ds(h, decode, stride=heads), :].astype(BF16)

    own_rows = mine_hbm.shape[0]
    core = core_ref[0]
    first = pl.multiple_of(core * own_rows, 8)
    second = pl.multiple_of((1 - core) * own_rows, 8)
    a = att[...]
    leaving = []
    for i in range(pieces):
        weights[i].wait()
        cs = pl.ds(i * step, step)
        acc[:, cs] = dot(a, wo_buf[:, cs])
        for n, (at, dst) in enumerate(((second, other_hbm), (first, mine_hbm))):
            c = pltpu.make_async_copy(acc.at[pl.ds(at, own_rows), cs], dst.at[:, cs], sem.at[4 + n, i])
            c.start()
            leaving.append(c)
    for c in leaving:
        c.wait()


def attend(lens, core, q, fk, fv, ck, cv, wo):
    rows, width = q.shape
    requests, slots, kvw = ck.shape
    heads = width // HEAD
    pairs = (requests - 1) * heads
    own = rows // 2
    sm = pl.BlockSpec(memory_space=pltpu.SMEM)
    hb = pl.BlockSpec(memory_space=pl.ANY)
    out = jax.ShapeDtypeStruct((own, wo.shape[1]), F32)
    return pl.pallas_call(
        attend_kernel,
        name="attend",
        out_shape=(out, out),
        in_specs=[sm, sm] + [hb] * 6,
        out_specs=(hb, hb),
        scratch_shapes=[
            VMEM(q.shape, BF16),
            VMEM(fk.shape, BF16),
            VMEM(fv.shape, BF16),
            VMEM(ck.shape, BF16),
            VMEM(cv.shape, BF16),
            VMEM(wo.shape, BF16),
            VMEM((rows, width), BF16),
            VMEM((rows, wo.shape[1]), F32),
            VMEM((pairs, HEAD), F32),
            VMEM((pairs, HEAD), F32),
            VMEM((pairs, HEAD), F32),
            VMEM((pairs, slots), F32),
            VMEM((pairs, HEAD), F32),
            pltpu.SemaphoreType.DMA((6, 4)),
        ],
        compiler_params=pltpu.CompilerParams(vmem_limit_bytes=FULL),
    )(lens, core, q, fk, fv, ck, cv, wo)


MAIN = 8


def spread_last(scr, rows):
    tiles = scr.shape[0]
    for q in range(MAIN):
        for j in range(tiles):
            at = (q * tiles + j) * HEAD
            scr[j, pl.ds(q, rows.shape[0], stride=MAIN), :] = rows[:, at : at + HEAD]
    return jnp.concatenate([scr[j] for j in range(tiles)], 1).astype(BF16)


def collect_last(scr, pieces, count):
    tiles = scr.shape[0]
    pieces = pieces.astype(F32)
    for j in range(tiles):
        scr[j] = pieces[:, j * HEAD : (j + 1) * HEAD]
    rows = [scr[j, pl.ds(q, count, stride=MAIN), :] for q in range(MAIN) for j in range(tiles)]
    return jnp.concatenate(rows, 1).astype(BF16)


def last_scratch(rows, width):
    return VMEM((width // MAIN // HEAD, rows, HEAD), F32)


def expander(experts):
    shape = (experts, experts * MAIN)
    return ((iota(shape, 1) >> 3) == iota(shape, 0)).astype(F32).astype(BF16)


def route_kernel(
    base_ref, recv_ref, router_ref, gain_ref, ids_ref, live_ref,
    hidden_ref, gate_ref, rank_ref, send_ref, scr,
):
    rows, width = base_ref.shape
    experts = router_ref.shape[1]
    hidden = (base_ref[...] + recv_ref[...]).astype(BF16)
    hidden_ref[...] = hidden
    h32 = hidden.astype(F32)
    mean = jnp.mean(h32 * h32, -1, keepdims=True)
    normed = (h32 * lax.rsqrt(mean + NORM_EPS) * gain_ref[...].astype(F32)).astype(BF16)
    logits = dot(normed, router_ref[...])
    lane = iota((rows, experts), 1)
    ids = ids_ref[...]
    chosen = ids[:, 0:1] == lane
    for k in range(1, ids.shape[1]):
        chosen = chosen | (ids[:, k : k + 1] == lane)
    raised = jnp.where(chosen, jnp.exp(jnp.where(chosen, logits, 0.0)), 0.0)
    gate_ref[...] = raised / jnp.sum(raised, -1, keepdims=True)
    used = jnp.where(chosen & (live_ref[...] > 0), 1.0, 0.0)
    before = (iota((rows, rows), 0) > iota((rows, rows), 1)).astype(F32).astype(BF16)
    rank = used * (dot(before, used.astype(BF16)) + 1.0)
    rank_ref[...] = rank
    spread = dot(rank.astype(BF16), expander(experts))
    slot = (iota(spread.shape, 1) & (MAIN - 1)).astype(F32) + 1.0
    pick = jnp.where(spread == slot, 1.0, 0.0).astype(BF16)
    block = width // 4
    for n in range(4):
        cs = slice(n * block, (n + 1) * block)
        send_ref[:, cs] = dot_tn(pick, normed[:, cs]).astype(BF16)
    last = jnp.where(rank == MAIN + 1.0, 1.0, 0.0).astype(BF16)
    send_ref[:, width:] = spread_last(scr, dot_tn(last, normed))


def route(base, recv, router, gain, ids, live):
    rows, width = base.shape
    experts = router.shape[1]
    part = width // MAIN
    vm = pl.BlockSpec(memory_space=VMEM)
    return pl.pallas_call(
        route_kernel,
        name="route",
        out_shape=(
            jax.ShapeDtypeStruct((rows, width), BF16),
            jax.ShapeDtypeStruct((rows, experts), F32),
            jax.ShapeDtypeStruct((rows, experts), F32),
            jax.ShapeDtypeStruct((experts * MAIN, width + part), BF16),
        ),
        in_specs=[vm] * 6,
        out_specs=(vm,) * 4,
        scratch_shapes=[last_scratch(experts * MAIN, width)],
        compiler_params=pltpu.CompilerParams(vmem_limit_bytes=LIMIT),
    )(base, recv, router, gain, ids, live)


def expert_kernel(x_ref, wg_ref, wu_ref, wd_ref, y_ref, scr):
    wg, wu, wd = wg_ref.at[0], wu_ref.at[0], wd_ref.at[0]
    width = wg.shape[0]

    def mlp(x):
        g = dot(x, wg[...])
        u = dot(x, wu[...])
        return dot((g * jax.nn.sigmoid(g) * u).astype(BF16), wd[...])

    count = x_ref.shape[0]
    last = collect_last(scr, x_ref[:, width:], count // MAIN)
    y_ref[:, width:] = spread_last(scr, mlp(last))
    chunk = 256

    @pl.loop(0, count // chunk)
    def _(i):
        rows = pl.ds(pl.multiple_of(i * chunk, chunk), chunk)
        y_ref[rows, :width] = mlp(x_ref[rows, :width]).astype(BF16)


def expert(x, wg, wu, wd):
    vm = pl.BlockSpec(memory_space=VMEM)
    return pl.pallas_call(
        expert_kernel,
        name="expert",
        out_shape=jax.ShapeDtypeStruct(x.shape, BF16),
        in_specs=[vm] * 4,
        out_specs=vm,
        scratch_shapes=[last_scratch(x.shape[0], wg.shape[1])],
        compiler_params=pltpu.CompilerParams(vmem_limit_bytes=LIMIT),
    )(x, wg, wu, wd)


def combine_kernel(hidden_ref, gate_ref, rank_ref, y_ref, out_ref, scr):
    rows, width = hidden_ref.shape
    experts = gate_ref.shape[1]
    rank = rank_ref[...]
    gate = gate_ref[...]
    high = gate.astype(BF16).astype(F32)
    both = jnp.concatenate([high, gate - high], 0)
    rank2 = jnp.concatenate([rank, rank], 0)
    grow = expander(experts)
    spread = dot(rank2.astype(BF16), grow)
    slot = (iota(spread.shape, 1) & (MAIN - 1)).astype(F32) + 1.0
    main = jnp.where(spread == slot, dot(both.astype(BF16), grow), 0.0).astype(BF16)
    last = jnp.where(rank2 == MAIN + 1.0, both, 0.0).astype(BF16)
    tail = collect_last(scr, y_ref[:, width:], experts)
    block = width // 4
    for n in range(4):
        cs = slice(n * block, (n + 1) * block)
        mix = dot(main, y_ref[:, cs]) + dot(last, tail[:, cs])
        out_ref[:, cs] = (hidden_ref[:, cs].astype(F32) + (mix[:rows] + mix[rows:])).astype(BF16)


def combine(hidden, gate, rank, y):
    vm = pl.BlockSpec(memory_space=VMEM)
    return pl.pallas_call(
        combine_kernel,
        name="combine",
        out_shape=jax.ShapeDtypeStruct(hidden.shape, BF16),
        in_specs=[vm] * 4,
        out_specs=vm,
        scratch_shapes=[last_scratch(y.shape[0], hidden.shape[1])],
        compiler_params=pltpu.CompilerParams(vmem_limit_bytes=LIMIT),
    )(hidden, gate, rank, y)


def exchange(x, experts):
    blocks = x.reshape(experts, MAIN, x.shape[1])
    moved = lax.all_to_all(blocks, ("ep", "dp"), split_axis=0, concat_axis=0, tiled=True)
    return moved.reshape(x.shape)


def on_device(
    residual, queries, fresh_rotated_keys, fresh_values, cache_keys, request_value_cache,
    cache_lengths, out_proj, router_weight, norm_gain, expert_ids, live_mask,
    w_gate, w_up, w_down,
):
    experts = router_weight.shape[1]
    core = lax.axis_index("dp").astype(jnp.int32).reshape(1)
    mine, other = attend(
        cache_lengths, core, queries, fresh_rotated_keys, fresh_values, cache_keys,
        request_value_cache, out_proj,
    )
    recv = lax.ppermute(other, "dp", [(0, 1), (1, 0)])
    hidden, gate, rank, send = route(
        residual.astype(F32) + mine, recv, router_weight, norm_gain.reshape(1, -1), expert_ids,
        live_mask.reshape(-1, 1),
    )
    back = exchange(expert(exchange(send, experts), w_gate, w_up, w_down), experts)
    return combine(hidden, gate, rank, back)


def solution(mesh):
    both = ("ep", "dp")
    placed = (
        P(both, None),
        P("ep", "dp"),
        P("ep", "dp"),
        P("ep", "dp"),
        P("ep", None, "dp"),
        P("ep", None, "dp"),
        P("ep"),
        P("dp", None),
        P(),
        P(),
        P(both, None),
        P(both),
        P(both, None, None),
        P(both, None, None),
        P(both, None, None),
    )
    return jax.shard_map(
        on_device, mesh=mesh, in_specs=placed, out_specs=P(both, None), check_vma=False
    )
```

```python
import math

import jax
import jax.numpy as jnp
from jax import lax
from jax.experimental import pallas as pl
from jax.experimental.pallas import tpu as pltpu
from jax.sharding import PartitionSpec as P

HEAD = 128
NEG_FILL = -1e30
NORM_EPS = 1e-06
F32 = jnp.float32
BF16 = jnp.bfloat16
VMEM = pltpu.VMEM
LIMIT = 30 * 1024 * 1024
FULL = 60 * 1024 * 1024


def dot(a, b):
    return jnp.dot(a, b, preferred_element_type=F32)


def dot_nt(a, b):
    return lax.dot_general(a, b, (((1,), (1,)), ((), ())), preferred_element_type=F32)


def dot_tn(a, b):
    return lax.dot_general(a, b, (((0,), (0,)), ((), ())), preferred_element_type=F32)


def iota(shape, axis):
    return lax.broadcasted_iota(jnp.int32, shape, axis)


def softmax_parts(scores):
    top = jnp.max(scores, -1, keepdims=True)
    raised = jnp.exp(scores - top)
    return raised, jnp.sum(raised, -1, keepdims=True)


def attend_kernel(
    lens_ref, core_ref, q_hbm, fk_hbm, fv_hbm, ck_hbm, cv_hbm, wo_hbm,
    mine_hbm, other_hbm,
    q_ref, fk_ref, fv_ref, k_buf, v_buf, wo_buf, att, acc, dq, dk, dv, ds, do, sem,
):
    rows, width = q_ref.shape
    requests, slots, kvw = k_buf.shape
    decode = requests - 1
    span = rows - decode
    kvh = kvw // HEAD
    heads = width // HEAD
    per = heads // kvh
    scale = 1.0 / math.sqrt(HEAD)
    half = requests // 2 + 1

    cuts = ((0, 1), (1, half), (half, requests))
    copies = []
    for i, (lo, hi) in enumerate(cuts):
        copies.append(pltpu.make_async_copy(ck_hbm.at[pl.ds(lo, hi - lo)], k_buf.at[pl.ds(lo, hi - lo)], sem.at[0, i]))
        copies.append(pltpu.make_async_copy(cv_hbm.at[pl.ds(lo, hi - lo)], v_buf.at[pl.ds(lo, hi - lo)], sem.at[1, i]))
    pieces = 4
    step = wo_buf.shape[1] // pieces
    weights = [
        pltpu.make_async_copy(wo_hbm.at[:, pl.ds(i * step, step)], wo_buf.at[:, pl.ds(i * step, step)], sem.at[2, i])
        for i in range(pieces)
    ]
    small = [
        pltpu.make_async_copy(src, dst, sem.at[3, i])
        for i, (src, dst) in enumerate(((q_hbm, q_ref), (fk_hbm, fk_ref), (fv_hbm, fv_ref)))
    ]
    for c in small + copies + weights:
        c.start()
    for c in small:
        c.wait()

    tail = q_ref[span:, :].astype(F32)
    tail_k = fk_ref[span:, :].astype(F32)
    tail_v = fv_ref[span:, :].astype(F32)
    for h in range(heads):
        g = h // per
        dq[pl.ds(h, decode, stride=heads), :] = tail[:, h * HEAD : (h + 1) * HEAD]
        dk[pl.ds(h, decode, stride=heads), :] = tail_k[:, g * HEAD : (g + 1) * HEAD]
        dv[pl.ds(h, decode, stride=heads), :] = tail_v[:, g * HEAD : (g + 1) * HEAD]

    copies[0].wait()
    copies[1].wait()
    total = slots + span
    shape = (per * span, total)
    col = iota(shape, 1)
    place = iota(shape, 0) & (span - 1)
    allowed = ((col < slots) & (col < lens_ref[0])) | ((col >= slots) & (col - slots <= place))
    for g in range(kvh):
        gs = slice(g * HEAD, (g + 1) * HEAD)
        q = jnp.concatenate(
            [q_ref[:span, (g * per + j) * HEAD : (g * per + j + 1) * HEAD] for j in range(per)], 0
        )
        k = jnp.concatenate([k_buf[0, :, gs], fk_ref[:span, gs]], 0)
        v = jnp.concatenate([v_buf[0, :, gs], fv_ref[:span, gs]], 0)
        s = jnp.where(allowed, dot_nt(q, k) * scale, NEG_FILL)
        raised, norm = softmax_parts(s)
        p = (raised * (1.0 / norm)).astype(BF16)
        o = dot(p, v).astype(BF16)
        for j in range(per):
            h = g * per + j
            att[:span, h * HEAD : (h + 1) * HEAD] = o[j * span : (j + 1) * span]

    pairs = decode * heads
    lower = (iota((pairs, HEAD), 0) & (heads - 1)) < per
    qv = dq[...]
    qbd = jnp.concatenate([jnp.where(lower, qv, 0.0), jnp.where(lower, 0.0, qv)], 1).astype(BF16)
    own = jnp.sum(qv * dk[...], -1, keepdims=True) * scale
    lane = iota((heads, slots), 1)
    for r in range(decode):
        if r == 0:
            copies[2].wait()
        if r + 1 == half:
            copies[4].wait()
        s = dot_nt(qbd[r * heads : (r + 1) * heads], k_buf[r + 1]) * scale
        ds[r * heads : (r + 1) * heads, :] = jnp.where(lane < lens_ref[r + 1], s, NEG_FILL)
    s = ds[...]
    top = jnp.maximum(jnp.max(s, -1, keepdims=True), own)
    raised = jnp.exp(s - top)
    own_raised = jnp.exp(own - top)
    inv = 1.0 / (jnp.sum(raised, -1, keepdims=True) + own_raised)
    p = (raised * inv).astype(BF16)
    own_p = (own_raised * inv).astype(BF16).astype(F32)
    copies[3].wait()
    copies[5].wait()
    for r in range(decode):
        o = dot(p[r * heads : (r + 1) * heads], v_buf[r + 1])
        do[r * heads : r * heads + per, :] = o[:per, :HEAD]
        do[r * heads + per : (r + 1) * heads, :] = o[per:, HEAD:]
    do[...] = do[...] + own_p * dv[...]
    for h in range(heads):
        att[span:, h * HEAD : (h + 1) * HEAD] = do[pl.ds(h, decode, stride=heads), :].astype(BF16)

    own_rows = mine_hbm.shape[0]
    core = core_ref[0]
    first = pl.multiple_of(core * own_rows, 8)
    second = pl.multiple_of((1 - core) * own_rows, 8)
    a = att[...]
    leaving = []
    for i in range(pieces):
        weights[i].wait()
        cs = pl.ds(i * step, step)
        acc[:, cs] = dot(a, wo_buf[:, cs])
        for n, (at, dst) in enumerate(((second, other_hbm), (first, mine_hbm))):
            c = pltpu.make_async_copy(acc.at[pl.ds(at, own_rows), cs], dst.at[:, cs], sem.at[4 + n, i])
            c.start()
            leaving.append(c)
    for c in leaving:
        c.wait()


def attend(lens, core, q, fk, fv, ck, cv, wo):
    rows, width = q.shape
    requests, slots, kvw = ck.shape
    heads = width // HEAD
    pairs = (requests - 1) * heads
    own = rows // 2
    sm = pl.BlockSpec(memory_space=pltpu.SMEM)
    hb = pl.BlockSpec(memory_space=pl.ANY)
    out = jax.ShapeDtypeStruct((own, wo.shape[1]), F32)
    return pl.pallas_call(
        attend_kernel,
        name="attend",
        out_shape=(out, out),
        in_specs=[sm, sm] + [hb] * 6,
        out_specs=(hb, hb),
        scratch_shapes=[
            VMEM(q.shape, BF16),
            VMEM(fk.shape, BF16),
            VMEM(fv.shape, BF16),
            VMEM(ck.shape, BF16),
            VMEM(cv.shape, BF16),
            VMEM(wo.shape, BF16),
            VMEM((rows, width), BF16),
            VMEM((rows, wo.shape[1]), F32),
            VMEM((pairs, HEAD), F32),
            VMEM((pairs, HEAD), F32),
            VMEM((pairs, HEAD), F32),
            VMEM((pairs, slots), F32),
            VMEM((pairs, HEAD), F32),
            pltpu.SemaphoreType.DMA((6, 4)),
        ],
        compiler_params=pltpu.CompilerParams(vmem_limit_bytes=FULL),
    )(lens, core, q, fk, fv, ck, cv, wo)


MAIN = 8


CHUNK = 320
GROUPS = 4
WINDOW = 128
MARK = 1e-36


def spread_last(scr, rows):
    tiles = scr.shape[0]
    for q in range(MAIN):
        for j in range(tiles):
            at = (q * tiles + j) * HEAD
            scr[j, pl.ds(q, rows.shape[0], stride=MAIN), :] = rows[:, at : at + HEAD]
    return jnp.concatenate([scr[j] for j in range(tiles)], 1).astype(BF16)


def collect_last(scr, pieces, count):
    tiles = scr.shape[0]
    pieces = pieces.astype(F32)
    for j in range(tiles):
        scr[j] = pieces[:, j * HEAD : (j + 1) * HEAD]
    rows = [scr[j, pl.ds(q, count, stride=MAIN), :] for q in range(MAIN) for j in range(tiles)]
    return jnp.concatenate(rows, 1).astype(BF16)


def last_scratch(rows, width):
    return VMEM((width // MAIN // HEAD, rows, HEAD), F32)


def expander(experts):
    shape = (experts, experts * MAIN)
    return ((iota(shape, 1) >> 3) == iota(shape, 0)).astype(F32).astype(BF16)


def route_kernel(
    base_ref, recv_ref, router_ref, gain_ref, ids_ref, live_ref,
    hidden_ref, gate_ref, rank_ref, send_ref, scr,
):
    rows, width = base_ref.shape
    experts = router_ref.shape[1]
    hidden = (base_ref[...] + recv_ref[...]).astype(BF16)
    hidden_ref[...] = hidden
    h32 = hidden.astype(F32)
    mean = jnp.mean(h32 * h32, -1, keepdims=True)
    normed = (h32 * lax.rsqrt(mean + NORM_EPS) * gain_ref[...].astype(F32)).astype(BF16)
    logits = dot(normed, router_ref[...])
    lane = iota((rows, experts), 1)
    ids = ids_ref[...]
    chosen = ids[:, 0:1] == lane
    for k in range(1, ids.shape[1]):
        chosen = chosen | (ids[:, k : k + 1] == lane)
    raised = jnp.where(chosen, jnp.exp(jnp.where(chosen, logits, 0.0)), 0.0)
    gate_ref[...] = raised / jnp.sum(raised, -1, keepdims=True)
    used = jnp.where(chosen & (live_ref[...] > 0), 1.0, 0.0)
    before = (iota((rows, rows), 0) > iota((rows, rows), 1)).astype(F32).astype(BF16)
    rank = used * (dot(before, used.astype(BF16)) + 1.0)
    rank_ref[...] = rank
    spread = dot(rank.astype(BF16), expander(experts))
    slot = (iota(spread.shape, 1) & (MAIN - 1)).astype(F32) + 1.0
    pick = jnp.where(spread == slot, 1.0, 0.0).astype(BF16)
    head = normed[:, :HEAD].astype(F32)
    head = jnp.where((iota(head.shape, 1) == 0) & (head == 0.0), MARK, head).astype(BF16)
    normed = jnp.concatenate([head, normed[:, HEAD:]], 1)
    block = width // 4
    for n in range(4):
        cs = slice(n * block, (n + 1) * block)
        send_ref[:, cs] = dot_tn(pick, normed[:, cs]).astype(BF16)
    last = jnp.where(rank == MAIN + 1.0, 1.0, 0.0).astype(BF16)
    send_ref[:, width:] = spread_last(scr, dot_tn(last, normed))


def route(base, recv, router, gain, ids, live):
    rows, width = base.shape
    experts = router.shape[1]
    part = width // MAIN
    vm = pl.BlockSpec(memory_space=VMEM)
    return pl.pallas_call(
        route_kernel,
        name="route",
        out_shape=(
            jax.ShapeDtypeStruct((rows, width), BF16),
            jax.ShapeDtypeStruct((rows, experts), F32),
            jax.ShapeDtypeStruct((rows, experts), F32),
            jax.ShapeDtypeStruct((experts * MAIN, width + part), BF16),
        ),
        in_specs=[vm] * 6,
        out_specs=(vm,) * 4,
        scratch_shapes=[last_scratch(experts * MAIN, width)],
        compiler_params=pltpu.CompilerParams(vmem_limit_bytes=LIMIT),
    )(base, recv, router, gain, ids, live)


def in_use(rows):
    used = jnp.where((iota(rows.shape, 1) == 0) & (rows.astype(F32) != 0.0), 1.0, 0.0)
    return dot_nt(jnp.ones((8, HEAD), BF16), used.astype(BF16))


def places(main, last):
    sources = last.shape[1]
    grow = expander(sources)
    slot = iota(main.shape, 1) & (MAIN - 1)
    upto = main
    for shift in (1, 2, 4):
        upto = upto + jnp.where(slot >= shift, pltpu.roll(upto, shift, 1), 0.0)
    count = dot_nt(main.astype(BF16), grow)
    held = count + last
    before = (iota((sources, sources), 0) < iota((sources, sources), 1)).astype(F32).astype(BF16)
    base = dot(held.astype(BF16), before)
    high = jnp.floor(base * (1.0 / 64.0))
    parts = dot(jnp.concatenate([high, base - 64.0 * high], 0).astype(BF16), grow)
    first = 64.0 * parts[:8] + parts[8:]
    at_main = jnp.where(main > 0.0, first + upto - 1.0, -1.0)
    at_last = jnp.where(last > 0.0, base + count, -1.0)
    return at_main, at_last, base[0:1], jnp.sum(held[0:1]).astype(jnp.int32)


def expert_kernel(x_ref, wg_ref, wu_ref, wd_ref, y_ref, scr, x_buf, y_buf):
    wg, wu, wd = wg_ref.at[0], wu_ref.at[0], wd_ref.at[0]
    width = wg.shape[0]
    count = x_ref.shape[0]
    sources = count // MAIN
    last = collect_last(scr, x_ref[:, width:], sources)
    at_main, at_last, base, total = places(in_use(x_ref[:, :HEAD]), in_use(last[:, :HEAD]))
    block = width // 4
    members = sources // GROUPS
    lane = iota(base.shape, 1)
    edges = [
        jnp.sum(jnp.where(lane == j * members, base, 0.0)).astype(jnp.int32) for j in range(GROUPS)
    ] + [total]
    starts = [e & ~15 for e in edges[:-1]]
    fits = total <= CHUNK
    for j in range(GROUPS):
        fits = fits & (edges[j + 1] - starts[j] <= WINDOW)

    def mlp(x):
        g = dot(x, wg[...])
        u = dot(x, wu[...])
        return dot((g * jax.nn.sigmoid(g) * u).astype(BF16), wd[...])

    def hot(at, rows, start):
        row = iota((rows, at.shape[1]), 0) + start
        return jnp.where(at[0:1].astype(jnp.int32) == row, 1.0, 0.0).astype(BF16)

    @pl.when(fits)
    def _():
        main, tail = hot(at_main, CHUNK, 0), hot(at_last, CHUNK, 0)
        for n in range(4):
            cs = slice(n * block, (n + 1) * block)
            x_buf[:, cs] = (dot(main, x_ref[:, cs]) + dot(tail, last[:, cs])).astype(BF16)
        y_buf[:CHUNK, :] = mlp(x_buf[...]).astype(BF16)
        y_buf[CHUNK:, :] = jnp.zeros((WINDOW, width), BF16)
        size = members * MAIN
        for j in range(GROUPS):
            rows = slice(j * size, (j + 1) * size)
            near = hot(at_main[:, rows], WINDOW, starts[j])
            from_ = pl.ds(pl.multiple_of(starts[j], 16), WINDOW)
            for n in range(4):
                cs = slice(n * block, (n + 1) * block)
                y_ref[rows, cs] = dot_tn(near, y_buf[from_, cs]).astype(BF16)
        y_ref[:, width:] = spread_last(scr, dot_tn(tail, y_buf[:CHUNK, :]))

    @pl.when(jnp.logical_not(fits))
    def _():
        y_ref[:, width:] = spread_last(scr, mlp(last))
        step = 256

        @pl.loop(0, count // step)
        def _(i):
            rows = pl.ds(pl.multiple_of(i * step, step), step)
            y_ref[rows, :width] = mlp(x_ref[rows, :width]).astype(BF16)


def expert(x, wg, wu, wd):
    vm = pl.BlockSpec(memory_space=VMEM)
    width = wg.shape[1]
    return pl.pallas_call(
        expert_kernel,
        name="expert",
        out_shape=jax.ShapeDtypeStruct(x.shape, BF16),
        in_specs=[vm] * 4,
        out_specs=vm,
        scratch_shapes=[
            last_scratch(x.shape[0], width),
            VMEM((CHUNK, width), BF16),
            VMEM((CHUNK + WINDOW, width), BF16),
        ],
        compiler_params=pltpu.CompilerParams(vmem_limit_bytes=LIMIT),
    )(x, wg, wu, wd)


def combine_kernel(hidden_ref, gate_ref, rank_ref, y_ref, out_ref, scr):
    rows, width = hidden_ref.shape
    experts = gate_ref.shape[1]
    rank = rank_ref[...]
    gate = gate_ref[...]
    high = gate.astype(BF16).astype(F32)
    both = jnp.concatenate([high, gate - high], 0)
    rank2 = jnp.concatenate([rank, rank], 0)
    grow = expander(experts)
    spread = dot(rank2.astype(BF16), grow)
    slot = (iota(spread.shape, 1) & (MAIN - 1)).astype(F32) + 1.0
    main = jnp.where(spread == slot, dot(both.astype(BF16), grow), 0.0).astype(BF16)
    last = jnp.where(rank2 == MAIN + 1.0, both, 0.0).astype(BF16)
    tail = collect_last(scr, y_ref[:, width:], experts)
    block = width // 4
    for n in range(4):
        cs = slice(n * block, (n + 1) * block)
        mix = dot(main, y_ref[:, cs]) + dot(last, tail[:, cs])
        out_ref[:, cs] = (hidden_ref[:, cs].astype(F32) + (mix[:rows] + mix[rows:])).astype(BF16)


def combine(hidden, gate, rank, y):
    vm = pl.BlockSpec(memory_space=VMEM)
    return pl.pallas_call(
        combine_kernel,
        name="combine",
        out_shape=jax.ShapeDtypeStruct(hidden.shape, BF16),
        in_specs=[vm] * 4,
        out_specs=vm,
        scratch_shapes=[last_scratch(y.shape[0], hidden.shape[1])],
        compiler_params=pltpu.CompilerParams(vmem_limit_bytes=LIMIT),
    )(hidden, gate, rank, y)


def exchange(x, experts):
    blocks = x.reshape(experts, MAIN, x.shape[1])
    moved = lax.all_to_all(blocks, ("ep", "dp"), split_axis=0, concat_axis=0, tiled=True)
    return moved.reshape(x.shape)


def on_device(
    residual, queries, fresh_rotated_keys, fresh_values, cache_keys, request_value_cache,
    cache_lengths, out_proj, router_weight, norm_gain, expert_ids, live_mask,
    w_gate, w_up, w_down,
):
    experts = router_weight.shape[1]
    core = lax.axis_index("dp").astype(jnp.int32).reshape(1)
    mine, other = attend(
        cache_lengths, core, queries, fresh_rotated_keys, fresh_values, cache_keys,
        request_value_cache, out_proj,
    )
    recv = lax.ppermute(other, "dp", [(0, 1), (1, 0)])
    hidden, gate, rank, send = route(
        residual.astype(F32) + mine, recv, router_weight, norm_gain.reshape(1, -1), expert_ids,
        live_mask.reshape(-1, 1),
    )
    back = exchange(expert(exchange(send, experts), w_gate, w_up, w_down), experts)
    return combine(hidden, gate, rank, back)


def solution(mesh):
    both = ("ep", "dp")
    placed = (
        P(both, None),
        P("ep", "dp"),
        P("ep", "dp"),
        P("ep", "dp"),
        P("ep", None, "dp"),
        P("ep", None, "dp"),
        P("ep"),
        P("dp", None),
        P(),
        P(),
        P(both, None),
        P(both),
        P(both, None, None),
        P(both, None, None),
        P(both, None, None),
    )
    return jax.shard_map(
        on_device, mesh=mesh, in_specs=placed, out_specs=P(both, None), check_vma=False
    )
```

```python
import math

import jax
import jax.numpy as jnp
from jax import lax
from jax.experimental import pallas as pl
from jax.experimental.pallas import tpu as pltpu
from jax.sharding import PartitionSpec as P

HEAD = 128
NEG_FILL = -1e30
NORM_EPS = 1e-06
F32 = jnp.float32
BF16 = jnp.bfloat16
VMEM = pltpu.VMEM
LIMIT = 30 * 1024 * 1024
FULL = 60 * 1024 * 1024


def dot(a, b):
    return jnp.dot(a, b, preferred_element_type=F32)


def dot_nt(a, b):
    return lax.dot_general(a, b, (((1,), (1,)), ((), ())), preferred_element_type=F32)


def dot_tn(a, b):
    return lax.dot_general(a, b, (((0,), (0,)), ((), ())), preferred_element_type=F32)


def iota(shape, axis):
    return lax.broadcasted_iota(jnp.int32, shape, axis)


def softmax_parts(scores):
    top = jnp.max(scores, -1, keepdims=True)
    raised = jnp.exp(scores - top)
    return raised, jnp.sum(raised, -1, keepdims=True)


def attend_kernel(
    lens_ref, core_ref, q_hbm, fk_hbm, fv_hbm, ck_hbm, cv_hbm, wo_hbm,
    mine_hbm, other_hbm,
    q_ref, fk_ref, fv_ref, k_buf, v_buf, wo_buf, att, acc, dq, dk, dv, ds, do, sem,
):
    rows, width = q_ref.shape
    requests, slots, kvw = k_buf.shape
    decode = requests - 1
    span = rows - decode
    kvh = kvw // HEAD
    heads = width // HEAD
    per = heads // kvh
    scale = 1.0 / math.sqrt(HEAD)
    half = requests // 2 + 1

    cuts = ((0, 1), (1, half), (half, requests))
    copies = []
    for i, (lo, hi) in enumerate(cuts):
        copies.append(pltpu.make_async_copy(ck_hbm.at[pl.ds(lo, hi - lo)], k_buf.at[pl.ds(lo, hi - lo)], sem.at[0, i]))
        copies.append(pltpu.make_async_copy(cv_hbm.at[pl.ds(lo, hi - lo)], v_buf.at[pl.ds(lo, hi - lo)], sem.at[1, i]))
    pieces = 4
    step = wo_buf.shape[1] // pieces
    weights = [
        pltpu.make_async_copy(wo_hbm.at[:, pl.ds(i * step, step)], wo_buf.at[:, pl.ds(i * step, step)], sem.at[2, i])
        for i in range(pieces)
    ]
    small = [
        pltpu.make_async_copy(src, dst, sem.at[3, i])
        for i, (src, dst) in enumerate(((q_hbm, q_ref), (fk_hbm, fk_ref), (fv_hbm, fv_ref)))
    ]
    for c in small + copies + weights:
        c.start()
    for c in small:
        c.wait()

    tail = q_ref[span:, :].astype(F32)
    tail_k = fk_ref[span:, :].astype(F32)
    tail_v = fv_ref[span:, :].astype(F32)
    for h in range(heads):
        g = h // per
        dq[pl.ds(h, decode, stride=heads), :] = tail[:, h * HEAD : (h + 1) * HEAD]
        dk[pl.ds(h, decode, stride=heads), :] = tail_k[:, g * HEAD : (g + 1) * HEAD]
        dv[pl.ds(h, decode, stride=heads), :] = tail_v[:, g * HEAD : (g + 1) * HEAD]

    copies[0].wait()
    copies[1].wait()
    total = slots + span
    shape = (per * span, total)
    col = iota(shape, 1)
    place = iota(shape, 0) & (span - 1)
    allowed = ((col < slots) & (col < lens_ref[0])) | ((col >= slots) & (col - slots <= place))
    for g in range(kvh):
        gs = slice(g * HEAD, (g + 1) * HEAD)
        q = jnp.concatenate(
            [q_ref[:span, (g * per + j) * HEAD : (g * per + j + 1) * HEAD] for j in range(per)], 0
        )
        k = jnp.concatenate([k_buf[0, :, gs], fk_ref[:span, gs]], 0)
        v = jnp.concatenate([v_buf[0, :, gs], fv_ref[:span, gs]], 0)
        s = jnp.where(allowed, dot_nt(q, k) * scale, NEG_FILL)
        raised, norm = softmax_parts(s)
        p = (raised * (1.0 / norm)).astype(BF16)
        o = dot(p, v).astype(BF16)
        for j in range(per):
            h = g * per + j
            att[:span, h * HEAD : (h + 1) * HEAD] = o[j * span : (j + 1) * span]

    pairs = decode * heads
    lower = (iota((pairs, HEAD), 0) & (heads - 1)) < per
    qv = dq[...]
    qbd = jnp.concatenate([jnp.where(lower, qv, 0.0), jnp.where(lower, 0.0, qv)], 1).astype(BF16)
    own = jnp.sum(qv * dk[...], -1, keepdims=True) * scale
    lane = iota((heads, slots), 1)
    for r in range(decode):
        if r == 0:
            copies[2].wait()
        if r + 1 == half:
            copies[4].wait()
        s = dot_nt(qbd[r * heads : (r + 1) * heads], k_buf[r + 1]) * scale
        ds[r * heads : (r + 1) * heads, :] = jnp.where(lane < lens_ref[r + 1], s, NEG_FILL)
    s = ds[...]
    top = jnp.maximum(jnp.max(s, -1, keepdims=True), own)
    raised = jnp.exp(s - top)
    own_raised = jnp.exp(own - top)
    inv = 1.0 / (jnp.sum(raised, -1, keepdims=True) + own_raised)
    p = (raised * inv).astype(BF16)
    own_p = (own_raised * inv).astype(BF16).astype(F32)
    copies[3].wait()
    copies[5].wait()
    for r in range(decode):
        o = dot(p[r * heads : (r + 1) * heads], v_buf[r + 1])
        do[r * heads : r * heads + per, :] = o[:per, :HEAD]
        do[r * heads + per : (r + 1) * heads, :] = o[per:, HEAD:]
    do[...] = do[...] + own_p * dv[...]
    for h in range(heads):
        att[span:, h * HEAD : (h + 1) * HEAD] = do[pl.ds(h, decode, stride=heads), :].astype(BF16)

    own_rows = mine_hbm.shape[0]
    core = core_ref[0]
    first = pl.multiple_of(core * own_rows, 8)
    second = pl.multiple_of((1 - core) * own_rows, 8)
    a = att[...]
    leaving = []
    for i in range(pieces):
        weights[i].wait()
        cs = pl.ds(i * step, step)
        acc[:, cs] = dot(a, wo_buf[:, cs])
        for n, (at, dst) in enumerate(((second, other_hbm), (first, mine_hbm))):
            c = pltpu.make_async_copy(acc.at[pl.ds(at, own_rows), cs], dst.at[:, cs], sem.at[4 + n, i])
            c.start()
            leaving.append(c)
    for c in leaving:
        c.wait()


def attend(lens, core, q, fk, fv, ck, cv, wo):
    rows, width = q.shape
    requests, slots, kvw = ck.shape
    heads = width // HEAD
    pairs = (requests - 1) * heads
    own = rows // 2
    sm = pl.BlockSpec(memory_space=pltpu.SMEM)
    hb = pl.BlockSpec(memory_space=pl.ANY)
    out = jax.ShapeDtypeStruct((own, wo.shape[1]), F32)
    return pl.pallas_call(
        attend_kernel,
        name="attend",
        out_shape=(out, out),
        in_specs=[sm, sm] + [hb] * 6,
        out_specs=(hb, hb),
        scratch_shapes=[
            VMEM(q.shape, BF16),
            VMEM(fk.shape, BF16),
            VMEM(fv.shape, BF16),
            VMEM(ck.shape, BF16),
            VMEM(cv.shape, BF16),
            VMEM(wo.shape, BF16),
            VMEM((rows, width), BF16),
            VMEM((rows, wo.shape[1]), F32),
            VMEM((pairs, HEAD), F32),
            VMEM((pairs, HEAD), F32),
            VMEM((pairs, HEAD), F32),
            VMEM((pairs, slots), F32),
            VMEM((pairs, HEAD), F32),
            pltpu.SemaphoreType.DMA((6, 4)),
        ],
        compiler_params=pltpu.CompilerParams(vmem_limit_bytes=FULL),
    )(lens, core, q, fk, fv, ck, cv, wo)


MAIN = 8


CHUNK = 288
GROUPS = 4
WINDOW = 128
MARK = 1e-36


def spread_last(scr, rows):
    tiles = scr.shape[0]
    for q in range(MAIN):
        for j in range(tiles):
            at = (q * tiles + j) * HEAD
            scr[j, pl.ds(q, rows.shape[0], stride=MAIN), :] = rows[:, at : at + HEAD]
    return jnp.concatenate([scr[j] for j in range(tiles)], 1).astype(BF16)


def collect_last(scr, pieces, count):
    tiles = scr.shape[0]
    pieces = pieces.astype(F32)
    for j in range(tiles):
        scr[j] = pieces[:, j * HEAD : (j + 1) * HEAD]
    rows = [scr[j, pl.ds(q, count, stride=MAIN), :] for q in range(MAIN) for j in range(tiles)]
    return jnp.concatenate(rows, 1).astype(BF16)


def last_scratch(rows, width):
    return VMEM((width // MAIN // HEAD, rows, HEAD), F32)


def expander(experts):
    shape = (experts, experts * MAIN)
    return ((iota(shape, 1) >> 3) == iota(shape, 0)).astype(F32).astype(BF16)


def prepare_kernel(
    res_ref, mine_ref, ids_ref, live_ref, base_ref, chosen_ref, rank_ref, pick_ref, last_ref
):
    rows = res_ref.shape[0]
    experts = rank_ref.shape[1]
    base_ref[...] = res_ref[...].astype(F32) + mine_ref[...]
    lane = iota((rows, experts), 1)
    ids = ids_ref[...]
    chosen = ids[:, 0:1] == lane
    for k in range(1, ids.shape[1]):
        chosen = chosen | (ids[:, k : k + 1] == lane)
    chosen_ref[...] = jnp.where(chosen, 1.0, 0.0)
    used = jnp.where(chosen & (live_ref[...] > 0), 1.0, 0.0)
    before = (iota((rows, rows), 0) > iota((rows, rows), 1)).astype(F32).astype(BF16)
    rank = used * (dot(before, used.astype(BF16)) + 1.0)
    rank_ref[...] = rank
    spread = dot(rank.astype(BF16), expander(experts))
    slot = (iota(spread.shape, 1) & (MAIN - 1)).astype(F32) + 1.0
    pick_ref[...] = jnp.where(spread == slot, 1.0, 0.0).astype(BF16)
    last_ref[...] = jnp.where(rank == MAIN + 1.0, 1.0, 0.0).astype(BF16)


def prepare(res, mine, ids, live, experts):
    rows, width = res.shape
    vm = pl.BlockSpec(memory_space=VMEM)
    return pl.pallas_call(
        prepare_kernel,
        name="prepare",
        out_shape=(
            jax.ShapeDtypeStruct((rows, width), F32),
            jax.ShapeDtypeStruct((rows, experts), F32),
            jax.ShapeDtypeStruct((rows, experts), F32),
            jax.ShapeDtypeStruct((rows, experts * MAIN), BF16),
            jax.ShapeDtypeStruct((rows, experts), BF16),
        ),
        in_specs=[vm] * 4,
        out_specs=(vm,) * 5,
        cost_estimate=pl.CostEstimate(flops=2 * rows * width, bytes_accessed=10 * rows * width, transcendentals=0),
        compiler_params=pltpu.CompilerParams(vmem_limit_bytes=LIMIT),
    )(res, mine, ids, live)


def route_kernel(
    base_ref, recv_ref, router_ref, gain_ref, chosen_ref, pick_ref, last_ref,
    hidden_ref, gate_ref, send_ref, scr,
):
    width = base_ref.shape[1]
    hidden = (base_ref[...] + recv_ref[...]).astype(BF16)
    hidden_ref[...] = hidden
    h32 = hidden.astype(F32)
    mean = jnp.mean(h32 * h32, -1, keepdims=True)
    normed = (h32 * lax.rsqrt(mean + NORM_EPS) * gain_ref[...].astype(F32)).astype(BF16)
    head = normed[:, :HEAD].astype(F32)
    head = jnp.where((iota(head.shape, 1) == 0) & (head == 0.0), MARK, head).astype(BF16)
    marked = jnp.concatenate([head, normed[:, HEAD:]], 1)
    pick = pick_ref[...]
    block = width // 4
    for n in range(4):
        cs = slice(n * block, (n + 1) * block)
        send_ref[:, cs] = dot_tn(pick, marked[:, cs]).astype(BF16)
    send_ref[:, width:] = spread_last(scr, dot_tn(last_ref[...], marked))
    logits = dot(normed, router_ref[...])
    chosen = chosen_ref[...] > 0.0
    raised = jnp.where(chosen, jnp.exp(jnp.where(chosen, logits, 0.0)), 0.0)
    gate_ref[...] = raised / jnp.sum(raised, -1, keepdims=True)


def route(base, recv, router, gain, chosen, pick, last):
    rows, width = base.shape
    experts = router.shape[1]
    part = width // MAIN
    vm = pl.BlockSpec(memory_space=VMEM)
    return pl.pallas_call(
        route_kernel,
        name="route",
        out_shape=(
            jax.ShapeDtypeStruct((rows, width), BF16),
            jax.ShapeDtypeStruct((rows, experts), F32),
            jax.ShapeDtypeStruct((experts * MAIN, width + part), BF16),
        ),
        in_specs=[vm] * 7,
        out_specs=(vm,) * 3,
        scratch_shapes=[last_scratch(experts * MAIN, width)],
        compiler_params=pltpu.CompilerParams(vmem_limit_bytes=LIMIT),
    )(base, recv, router, gain, chosen, pick, last)


def in_use(rows):
    used = jnp.where((iota(rows.shape, 1) == 0) & (rows.astype(F32) != 0.0), 1.0, 0.0)
    return dot_nt(jnp.ones((8, HEAD), BF16), used.astype(BF16))


def places(main, last):
    sources = last.shape[1]
    grow = expander(sources)
    slot = iota(main.shape, 1) & (MAIN - 1)
    upto = main
    for shift in (1, 2, 4):
        upto = upto + jnp.where(slot >= shift, pltpu.roll(upto, shift, 1), 0.0)
    count = dot_nt(main.astype(BF16), grow)
    held = count + last
    before = (iota((sources, sources), 0) < iota((sources, sources), 1)).astype(F32).astype(BF16)
    base = dot(held.astype(BF16), before)
    high = jnp.floor(base * (1.0 / 64.0))
    parts = dot(jnp.concatenate([high, base - 64.0 * high], 0).astype(BF16), grow)
    first = 64.0 * parts[:8] + parts[8:]
    at_main = jnp.where(main > 0.0, first + upto - 1.0, -1.0)
    at_last = jnp.where(last > 0.0, base + count, -1.0)
    return at_main, at_last, base[0:1], jnp.sum(held[0:1]).astype(jnp.int32)


def expert_kernel(x_ref, wg_ref, wu_ref, wd_ref, y_ref, scr, x_buf, y_buf):
    wg, wu, wd = wg_ref.at[0], wu_ref.at[0], wd_ref.at[0]
    width = wg.shape[0]
    count = x_ref.shape[0]
    sources = count // MAIN
    last = collect_last(scr, x_ref[:, width:], sources)
    at_main, at_last, base, total = places(in_use(x_ref[:, :HEAD]), in_use(last[:, :HEAD]))
    block = width // 4
    members = sources // GROUPS
    lane = iota(base.shape, 1)
    edges = [
        jnp.sum(jnp.where(lane == j * members, base, 0.0)).astype(jnp.int32) for j in range(GROUPS)
    ] + [total]
    starts = [e & ~15 for e in edges[:-1]]
    fits = total <= CHUNK
    for j in range(GROUPS):
        fits = fits & (edges[j + 1] - starts[j] <= WINDOW)

    def mlp(x):
        g = dot(x, wg[...])
        u = dot(x, wu[...])
        return dot((g * jax.nn.sigmoid(g) * u).astype(BF16), wd[...])

    def hot(at, rows, start):
        row = iota((rows, at.shape[1]), 0) + start
        return jnp.where(at[0:1].astype(jnp.int32) == row, 1.0, 0.0).astype(BF16)

    @pl.when(fits)
    def _():
        main, tail = hot(at_main, CHUNK, 0), hot(at_last, CHUNK, 0)
        for n in range(4):
            cs = slice(n * block, (n + 1) * block)
            x_buf[:, cs] = (dot(main, x_ref[:, cs]) + dot(tail, last[:, cs])).astype(BF16)
        y_buf[:CHUNK, :] = mlp(x_buf[...]).astype(BF16)
        y_buf[CHUNK:, :] = jnp.zeros((WINDOW, width), BF16)
        size = members * MAIN
        for j in range(GROUPS):
            rows = slice(j * size, (j + 1) * size)
            near = hot(at_main[:, rows], WINDOW, starts[j])
            from_ = pl.ds(pl.multiple_of(starts[j], 16), WINDOW)
            for n in range(4):
                cs = slice(n * block, (n + 1) * block)
                y_ref[rows, cs] = dot_tn(near, y_buf[from_, cs]).astype(BF16)
        y_ref[:, width:] = spread_last(scr, dot_tn(tail, y_buf[:CHUNK, :]))

    @pl.when(jnp.logical_not(fits))
    def _():
        y_ref[:, width:] = spread_last(scr, mlp(last))
        step = 256

        @pl.loop(0, count // step)
        def _(i):
            rows = pl.ds(pl.multiple_of(i * step, step), step)
            y_ref[rows, :width] = mlp(x_ref[rows, :width]).astype(BF16)


def expert(x, wg, wu, wd):
    vm = pl.BlockSpec(memory_space=VMEM)
    width = wg.shape[1]
    return pl.pallas_call(
        expert_kernel,
        name="expert",
        out_shape=jax.ShapeDtypeStruct(x.shape, BF16),
        in_specs=[vm] * 4,
        out_specs=vm,
        scratch_shapes=[
            last_scratch(x.shape[0], width),
            VMEM((CHUNK, width), BF16),
            VMEM((CHUNK + WINDOW, width), BF16),
        ],
        compiler_params=pltpu.CompilerParams(vmem_limit_bytes=LIMIT),
    )(x, wg, wu, wd)


def combine_kernel(hidden_ref, gate_ref, rank_ref, y_ref, out_ref, scr):
    rows, width = hidden_ref.shape
    experts = gate_ref.shape[1]
    rank = rank_ref[...]
    gate = gate_ref[...]
    high = gate.astype(BF16).astype(F32)
    both = jnp.concatenate([high, gate - high], 0)
    rank2 = jnp.concatenate([rank, rank], 0)
    grow = expander(experts)
    spread = dot(rank2.astype(BF16), grow)
    slot = (iota(spread.shape, 1) & (MAIN - 1)).astype(F32) + 1.0
    main = jnp.where(spread == slot, dot(both.astype(BF16), grow), 0.0).astype(BF16)
    last = jnp.where(rank2 == MAIN + 1.0, both, 0.0).astype(BF16)
    tail = collect_last(scr, y_ref[:, width:], experts)
    block = width // 4
    for n in range(4):
        cs = slice(n * block, (n + 1) * block)
        mix = dot(main, y_ref[:, cs]) + dot(last, tail[:, cs])
        out_ref[:, cs] = (hidden_ref[:, cs].astype(F32) + (mix[:rows] + mix[rows:])).astype(BF16)


def combine(hidden, gate, rank, y):
    vm = pl.BlockSpec(memory_space=VMEM)
    return pl.pallas_call(
        combine_kernel,
        name="combine",
        out_shape=jax.ShapeDtypeStruct(hidden.shape, BF16),
        in_specs=[vm] * 4,
        out_specs=vm,
        scratch_shapes=[last_scratch(y.shape[0], hidden.shape[1])],
        compiler_params=pltpu.CompilerParams(vmem_limit_bytes=LIMIT),
    )(hidden, gate, rank, y)


def exchange(x, experts):
    blocks = x.reshape(experts, MAIN, x.shape[1])
    moved = lax.all_to_all(blocks, ("ep", "dp"), split_axis=0, concat_axis=0, tiled=True)
    return moved.reshape(x.shape)


def on_device(
    residual, queries, fresh_rotated_keys, fresh_values, cache_keys, request_value_cache,
    cache_lengths, out_proj, router_weight, norm_gain, expert_ids, live_mask,
    w_gate, w_up, w_down,
):
    experts = router_weight.shape[1]
    core = lax.axis_index("dp").astype(jnp.int32).reshape(1)
    mine, other = attend(
        cache_lengths, core, queries, fresh_rotated_keys, fresh_values, cache_keys,
        request_value_cache, out_proj,
    )
    recv = lax.ppermute(other, "dp", [(0, 1), (1, 0)])
    base, chosen, rank, pick, last = prepare(
        residual, mine, expert_ids, live_mask.reshape(-1, 1), experts
    )
    hidden, gate, send = route(
        base, recv, router_weight, norm_gain.reshape(1, -1), chosen, pick, last
    )
    back = exchange(expert(exchange(send, experts), w_gate, w_up, w_down), experts)
    return combine(hidden, gate, rank, back)


def solution(mesh):
    both = ("ep", "dp")
    placed = (
        P(both, None),
        P("ep", "dp"),
        P("ep", "dp"),
        P("ep", "dp"),
        P("ep", None, "dp"),
        P("ep", None, "dp"),
        P("ep"),
        P("dp", None),
        P(),
        P(),
        P(both, None),
        P(both),
        P(both, None, None),
        P(both, None, None),
        P(both, None, None),
    )
    return jax.shard_map(
        on_device, mesh=mesh, in_specs=placed, out_specs=P(both, None), check_vma=False
    )
```

```python
import math

import jax
import jax.numpy as jnp
from jax import lax
from jax.experimental import pallas as pl
from jax.experimental.pallas import tpu as pltpu
from jax.sharding import PartitionSpec as P

HEAD = 128
NEG_FILL = -1e30
NORM_EPS = 1e-06
F32 = jnp.float32
BF16 = jnp.bfloat16
VMEM = pltpu.VMEM
LIMIT = 30 * 1024 * 1024
FULL = 52 * 1024 * 1024


def dot(a, b):
    return jnp.dot(a, b, preferred_element_type=F32)


def dot_nt(a, b):
    return lax.dot_general(a, b, (((1,), (1,)), ((), ())), preferred_element_type=F32)


def dot_tn(a, b):
    return lax.dot_general(a, b, (((0,), (0,)), ((), ())), preferred_element_type=F32)


def iota(shape, axis):
    return lax.broadcasted_iota(jnp.int32, shape, axis)


def softmax_parts(scores):
    top = jnp.max(scores, -1, keepdims=True)
    raised = jnp.exp(scores - top)
    return raised, jnp.sum(raised, -1, keepdims=True)


def attend_kernel(
    lens_ref, core_ref, q_hbm, fk_hbm, fv_hbm, ck_hbm, cv_hbm, wo_hbm,
    mine_hbm, other_hbm,
    q_ref, fk_ref, fv_ref, k_buf, v_buf, wo_buf, att, acc, dq, dk, dv, ds, do, sem,
):
    rows, width = q_ref.shape
    requests, slots, kvw = k_buf.shape
    decode = requests - 1
    span = rows - decode
    kvh = kvw // HEAD
    heads = width // HEAD
    per = heads // kvh
    scale = 1.0 / math.sqrt(HEAD)
    half = requests // 2 + 1

    cuts = ((0, 1), (1, half), (half, requests))
    copies = []
    for i, (lo, hi) in enumerate(cuts):
        copies.append(pltpu.make_async_copy(ck_hbm.at[pl.ds(lo, hi - lo)], k_buf.at[pl.ds(lo, hi - lo)], sem.at[0, i]))
        copies.append(pltpu.make_async_copy(cv_hbm.at[pl.ds(lo, hi - lo)], v_buf.at[pl.ds(lo, hi - lo)], sem.at[1, i]))
    pieces = 4
    step = wo_buf.shape[1] // pieces
    weights = [
        pltpu.make_async_copy(wo_hbm.at[:, pl.ds(i * step, step)], wo_buf.at[:, pl.ds(i * step, step)], sem.at[2, i])
        for i in range(pieces)
    ]
    small = [
        pltpu.make_async_copy(src, dst, sem.at[3, i])
        for i, (src, dst) in enumerate(((q_hbm, q_ref), (fk_hbm, fk_ref), (fv_hbm, fv_ref)))
    ]
    for c in small + copies + weights:
        c.start()
    for c in small:
        c.wait()

    tail = q_ref[span:, :].astype(F32)
    tail_k = fk_ref[span:, :].astype(F32)
    tail_v = fv_ref[span:, :].astype(F32)
    for h in range(heads):
        g = h // per
        dq[pl.ds(h, decode, stride=heads), :] = tail[:, h * HEAD : (h + 1) * HEAD]
        dk[pl.ds(h, decode, stride=heads), :] = tail_k[:, g * HEAD : (g + 1) * HEAD]
        dv[pl.ds(h, decode, stride=heads), :] = tail_v[:, g * HEAD : (g + 1) * HEAD]

    copies[0].wait()
    copies[1].wait()
    total = slots + span
    shape = (per * span, total)
    col = iota(shape, 1)
    place = iota(shape, 0) & (span - 1)
    allowed = ((col < slots) & (col < lens_ref[0])) | ((col >= slots) & (col - slots <= place))
    for g in range(kvh):
        gs = slice(g * HEAD, (g + 1) * HEAD)
        q = jnp.concatenate(
            [q_ref[:span, (g * per + j) * HEAD : (g * per + j + 1) * HEAD] for j in range(per)], 0
        )
        k = jnp.concatenate([k_buf[0, :, gs], fk_ref[:span, gs]], 0)
        v = jnp.concatenate([v_buf[0, :, gs], fv_ref[:span, gs]], 0)
        s = jnp.where(allowed, dot_nt(q, k) * scale, NEG_FILL)
        raised, norm = softmax_parts(s)
        p = (raised * (1.0 / norm)).astype(BF16)
        o = dot(p, v).astype(BF16)
        for j in range(per):
            h = g * per + j
            att[:span, h * HEAD : (h + 1) * HEAD] = o[j * span : (j + 1) * span]

    pairs = decode * heads
    lower = (iota((pairs, HEAD), 0) & (heads - 1)) < per
    qv = dq[...]
    qbd = jnp.concatenate([jnp.where(lower, qv, 0.0), jnp.where(lower, 0.0, qv)], 1).astype(BF16)
    own = jnp.sum(qv * dk[...], -1, keepdims=True) * scale
    lane = iota((heads, slots), 1)
    for r in range(decode):
        if r == 0:
            copies[2].wait()
        if r + 1 == half:
            copies[4].wait()
        s = dot_nt(qbd[r * heads : (r + 1) * heads], k_buf[r + 1]) * scale
        ds[r * heads : (r + 1) * heads, :] = jnp.where(lane < lens_ref[r + 1], s, NEG_FILL)
    s = ds[...]
    top = jnp.maximum(jnp.max(s, -1, keepdims=True), own)
    raised = jnp.exp(s - top)
    own_raised = jnp.exp(own - top)
    inv = 1.0 / (jnp.sum(raised, -1, keepdims=True) + own_raised)
    p = (raised * inv).astype(BF16)
    own_p = (own_raised * inv).astype(BF16).astype(F32)
    copies[3].wait()
    copies[5].wait()
    for r in range(decode):
        o = dot(p[r * heads : (r + 1) * heads], v_buf[r + 1])
        do[r * heads : r * heads + per, :] = o[:per, :HEAD]
        do[r * heads + per : (r + 1) * heads, :] = o[per:, HEAD:]
    do[...] = do[...] + own_p * dv[...]
    for h in range(heads):
        att[span:, h * HEAD : (h + 1) * HEAD] = do[pl.ds(h, decode, stride=heads), :].astype(BF16)

    own_rows = mine_hbm.shape[0]
    core = core_ref[0]
    first = pl.multiple_of(core * own_rows, 8)
    second = pl.multiple_of((1 - core) * own_rows, 8)
    a = att[...]
    leaving = []
    for i in range(pieces):
        weights[i].wait()
        cs = pl.ds(i * step, step)
        acc[:, cs] = dot(a, wo_buf[:, cs])
        for n, (at, dst) in enumerate(((second, other_hbm), (first, mine_hbm))):
            c = pltpu.make_async_copy(acc.at[pl.ds(at, own_rows), cs], dst.at[:, cs], sem.at[4 + n, i])
            c.start()
            leaving.append(c)
    for c in leaving:
        c.wait()


def attend(lens, core, q, fk, fv, ck, cv, wo):
    rows, width = q.shape
    requests, slots, kvw = ck.shape
    heads = width // HEAD
    pairs = (requests - 1) * heads
    own = rows // 2
    sm = pl.BlockSpec(memory_space=pltpu.SMEM)
    hb = pl.BlockSpec(memory_space=pl.ANY)
    out = jax.ShapeDtypeStruct((own, wo.shape[1]), F32)
    pinned = [pltpu.with_memory_space_constraint(a, pltpu.HBM) for a in (lens, q, fk, fv, ck, cv, wo)]
    return pl.pallas_call(
        attend_kernel,
        name="attend",
        out_shape=(out, out),
        in_specs=[sm, sm] + [hb] * 6,
        out_specs=(hb, hb),
        scratch_shapes=[
            VMEM(q.shape, BF16),
            VMEM(fk.shape, BF16),
            VMEM(fv.shape, BF16),
            VMEM(ck.shape, BF16),
            VMEM(cv.shape, BF16),
            VMEM(wo.shape, BF16),
            VMEM((rows, width), BF16),
            VMEM((rows, wo.shape[1]), F32),
            VMEM((pairs, HEAD), F32),
            VMEM((pairs, HEAD), F32),
            VMEM((pairs, HEAD), F32),
            VMEM((pairs, slots), F32),
            VMEM((pairs, HEAD), F32),
            pltpu.SemaphoreType.DMA((6, 4)),
        ],
        compiler_params=pltpu.CompilerParams(vmem_limit_bytes=FULL),
    )(pinned[0], core, *pinned[1:])


MAIN = 8


CHUNK = 288
GROUPS = 4
WINDOW = 128
MARK = 1e-36


def spread_last(scr, rows):
    tiles = scr.shape[0]
    for q in range(MAIN):
        for j in range(tiles):
            at = (q * tiles + j) * HEAD
            scr[j, pl.ds(q, rows.shape[0], stride=MAIN), :] = rows[:, at : at + HEAD]
    return jnp.concatenate([scr[j] for j in range(tiles)], 1).astype(BF16)


def collect_last(scr, pieces, count):
    tiles = scr.shape[0]
    pieces = pieces.astype(F32)
    for j in range(tiles):
        scr[j] = pieces[:, j * HEAD : (j + 1) * HEAD]
    rows = [scr[j, pl.ds(q, count, stride=MAIN), :] for q in range(MAIN) for j in range(tiles)]
    return jnp.concatenate(rows, 1).astype(BF16)


def last_scratch(rows, width):
    return VMEM((width // MAIN // HEAD, rows, HEAD), F32)


def expander(experts):
    shape = (experts, experts * MAIN)
    return ((iota(shape, 1) >> 3) == iota(shape, 0)).astype(F32).astype(BF16)


def prepare_kernel(
    res_ref, mine_ref, ids_ref, live_ref, base_ref, chosen_ref, rank_ref, pick_ref, last_ref
):
    rows = res_ref.shape[0]
    experts = rank_ref.shape[1]
    base_ref[...] = res_ref[...].astype(F32) + mine_ref[...]
    lane = iota((rows, experts), 1)
    ids = ids_ref[...]
    chosen = ids[:, 0:1] == lane
    for k in range(1, ids.shape[1]):
        chosen = chosen | (ids[:, k : k + 1] == lane)
    chosen_ref[...] = jnp.where(chosen, 1.0, 0.0)
    used = jnp.where(chosen & (live_ref[...] > 0), 1.0, 0.0)
    before = (iota((rows, rows), 0) > iota((rows, rows), 1)).astype(F32).astype(BF16)
    rank = used * (dot(before, used.astype(BF16)) + 1.0)
    rank_ref[...] = rank
    spread = dot(rank.astype(BF16), expander(experts))
    slot = (iota(spread.shape, 1) & (MAIN - 1)).astype(F32) + 1.0
    pick_ref[...] = jnp.where(spread == slot, 1.0, 0.0).astype(BF16)
    last_ref[...] = jnp.where(rank == MAIN + 1.0, 1.0, 0.0).astype(BF16)


def prepare(res, mine, ids, live, experts):
    rows, width = res.shape
    vm = pl.BlockSpec(memory_space=VMEM)
    return pl.pallas_call(
        prepare_kernel,
        name="prepare",
        out_shape=(
            jax.ShapeDtypeStruct((rows, width), F32),
            jax.ShapeDtypeStruct((rows, experts), F32),
            jax.ShapeDtypeStruct((rows, experts), F32),
            jax.ShapeDtypeStruct((rows, experts * MAIN), BF16),
            jax.ShapeDtypeStruct((rows, experts), BF16),
        ),
        in_specs=[vm] * 4,
        out_specs=(vm,) * 5,
        cost_estimate=pl.CostEstimate(flops=2 * rows * width, bytes_accessed=10 * rows * width, transcendentals=0),
        compiler_params=pltpu.CompilerParams(vmem_limit_bytes=LIMIT),
    )(res, mine, ids, live)


def route_kernel(
    base_ref, recv_ref, router_ref, gain_ref, chosen_ref, pick_ref, last_ref,
    hidden_ref, gate_ref, send_ref, scr,
):
    width = base_ref.shape[1]
    hidden = (base_ref[...] + recv_ref[...]).astype(BF16)
    hidden_ref[...] = hidden
    h32 = hidden.astype(F32)
    mean = jnp.mean(h32 * h32, -1, keepdims=True)
    normed = (h32 * lax.rsqrt(mean + NORM_EPS) * gain_ref[...].astype(F32)).astype(BF16)
    head = normed[:, :HEAD].astype(F32)
    head = jnp.where((iota(head.shape, 1) == 0) & (head == 0.0), MARK, head).astype(BF16)
    marked = jnp.concatenate([head, normed[:, HEAD:]], 1)
    pick = pick_ref[...]
    block = width // 4
    for n in range(4):
        cs = slice(n * block, (n + 1) * block)
        send_ref[:, cs] = dot_tn(pick, marked[:, cs]).astype(BF16)
    send_ref[:, width:] = spread_last(scr, dot_tn(last_ref[...], marked))
    logits = dot(normed, router_ref[...])
    chosen = chosen_ref[...] > 0.0
    raised = jnp.where(chosen, jnp.exp(jnp.where(chosen, logits, 0.0)), 0.0)
    gate_ref[...] = raised / jnp.sum(raised, -1, keepdims=True)


def route(base, recv, router, gain, chosen, pick, last):
    rows, width = base.shape
    experts = router.shape[1]
    part = width // MAIN
    vm = pl.BlockSpec(memory_space=VMEM)
    return pl.pallas_call(
        route_kernel,
        name="route",
        out_shape=(
            jax.ShapeDtypeStruct((rows, width), BF16),
            jax.ShapeDtypeStruct((rows, experts), F32),
            jax.ShapeDtypeStruct((experts * MAIN, width + part), BF16),
        ),
        in_specs=[vm] * 7,
        out_specs=(vm,) * 3,
        scratch_shapes=[last_scratch(experts * MAIN, width)],
        compiler_params=pltpu.CompilerParams(vmem_limit_bytes=LIMIT),
    )(base, recv, router, gain, chosen, pick, last)


def in_use(rows):
    used = jnp.where((iota(rows.shape, 1) == 0) & (rows.astype(F32) != 0.0), 1.0, 0.0)
    return dot_nt(jnp.ones((8, HEAD), BF16), used.astype(BF16))


def places(main, last):
    sources = last.shape[1]
    grow = expander(sources)
    slot = iota(main.shape, 1) & (MAIN - 1)
    upto = main
    for shift in (1, 2, 4):
        upto = upto + jnp.where(slot >= shift, pltpu.roll(upto, shift, 1), 0.0)
    count = dot_nt(main.astype(BF16), grow)
    held = count + last
    before = (iota((sources, sources), 0) < iota((sources, sources), 1)).astype(F32).astype(BF16)
    base = dot(held.astype(BF16), before)
    high = jnp.floor(base * (1.0 / 64.0))
    parts = dot(jnp.concatenate([high, base - 64.0 * high], 0).astype(BF16), grow)
    first = 64.0 * parts[:8] + parts[8:]
    at_main = jnp.where(main > 0.0, first + upto - 1.0, -1.0)
    at_last = jnp.where(last > 0.0, base + count, -1.0)
    return at_main, at_last, base[0:1], jnp.sum(held[0:1]).astype(jnp.int32)


def expert_kernel(x_ref, wg_ref, wu_ref, wd_ref, y_ref, scr, x_buf, y_buf):
    wg, wu, wd = wg_ref.at[0], wu_ref.at[0], wd_ref.at[0]
    width = wg.shape[0]
    count = x_ref.shape[0]
    sources = count // MAIN
    last = collect_last(scr, x_ref[:, width:], sources)
    at_main, at_last, base, total = places(in_use(x_ref[:, :HEAD]), in_use(last[:, :HEAD]))
    block = width // 4
    members = sources // GROUPS
    lane = iota(base.shape, 1)
    edges = [
        jnp.sum(jnp.where(lane == j * members, base, 0.0)).astype(jnp.int32) for j in range(GROUPS)
    ] + [total]
    starts = [e & ~15 for e in edges[:-1]]
    fits = total <= CHUNK
    for j in range(GROUPS):
        fits = fits & (edges[j + 1] - starts[j] <= WINDOW)

    def mlp(x):
        g = dot(x, wg[...])
        u = dot(x, wu[...])
        return dot((g * jax.nn.sigmoid(g) * u).astype(BF16), wd[...])

    def hot(at, rows, start):
        row = iota((rows, at.shape[1]), 0) + start
        return jnp.where(at[0:1].astype(jnp.int32) == row, 1.0, 0.0).astype(BF16)

    @pl.when(fits)
    def _():
        main, tail = hot(at_main, CHUNK, 0), hot(at_last, CHUNK, 0)
        for n in range(4):
            cs = slice(n * block, (n + 1) * block)
            x_buf[:, cs] = (dot(main, x_ref[:, cs]) + dot(tail, last[:, cs])).astype(BF16)
        y_buf[:CHUNK, :] = mlp(x_buf[...]).astype(BF16)
        y_buf[CHUNK:, :] = jnp.zeros((WINDOW, width), BF16)
        size = members * MAIN
        for j in range(GROUPS):
            rows = slice(j * size, (j + 1) * size)
            near = hot(at_main[:, rows], WINDOW, starts[j])
            from_ = pl.ds(pl.multiple_of(starts[j], 16), WINDOW)
            for n in range(4):
                cs = slice(n * block, (n + 1) * block)
                y_ref[rows, cs] = dot_tn(near, y_buf[from_, cs]).astype(BF16)
        y_ref[:, width:] = spread_last(scr, dot_tn(tail, y_buf[:CHUNK, :]))

    @pl.when(jnp.logical_not(fits))
    def _():
        y_ref[:, width:] = spread_last(scr, mlp(last))
        step = 256

        @pl.loop(0, count // step)
        def _(i):
            rows = pl.ds(pl.multiple_of(i * step, step), step)
            y_ref[rows, :width] = mlp(x_ref[rows, :width]).astype(BF16)


def expert(x, wg, wu, wd):
    vm = pl.BlockSpec(memory_space=VMEM)
    width = wg.shape[1]
    return pl.pallas_call(
        expert_kernel,
        name="expert",
        out_shape=jax.ShapeDtypeStruct(x.shape, BF16),
        in_specs=[vm] * 4,
        out_specs=vm,
        scratch_shapes=[
            last_scratch(x.shape[0], width),
            VMEM((CHUNK, width), BF16),
            VMEM((CHUNK + WINDOW, width), BF16),
        ],
        compiler_params=pltpu.CompilerParams(vmem_limit_bytes=LIMIT),
    )(x, wg, wu, wd)


def combine_kernel(hidden_ref, gate_ref, rank_ref, y_ref, out_ref, scr):
    rows, width = hidden_ref.shape
    experts = gate_ref.shape[1]
    rank = rank_ref[...]
    gate = gate_ref[...]
    high = gate.astype(BF16).astype(F32)
    both = jnp.concatenate([high, gate - high], 0)
    rank2 = jnp.concatenate([rank, rank], 0)
    grow = expander(experts)
    spread = dot(rank2.astype(BF16), grow)
    slot = (iota(spread.shape, 1) & (MAIN - 1)).astype(F32) + 1.0
    main = jnp.where(spread == slot, dot(both.astype(BF16), grow), 0.0).astype(BF16)
    last = jnp.where(rank2 == MAIN + 1.0, both, 0.0).astype(BF16)
    tail = collect_last(scr, y_ref[:, width:], experts)
    block = width // 4
    for n in range(4):
        cs = slice(n * block, (n + 1) * block)
        mix = dot(main, y_ref[:, cs]) + dot(last, tail[:, cs])
        out_ref[:, cs] = (hidden_ref[:, cs].astype(F32) + (mix[:rows] + mix[rows:])).astype(BF16)


def combine(hidden, gate, rank, y):
    vm = pl.BlockSpec(memory_space=VMEM)
    return pl.pallas_call(
        combine_kernel,
        name="combine",
        out_shape=jax.ShapeDtypeStruct(hidden.shape, BF16),
        in_specs=[vm] * 4,
        out_specs=vm,
        scratch_shapes=[last_scratch(y.shape[0], hidden.shape[1])],
        compiler_params=pltpu.CompilerParams(vmem_limit_bytes=LIMIT),
    )(hidden, gate, rank, y)


def exchange(x, experts):
    blocks = x.reshape(experts, MAIN, x.shape[1])
    moved = lax.all_to_all(blocks, ("ep", "dp"), split_axis=0, concat_axis=0, tiled=True)
    return moved.reshape(x.shape)


def on_device(
    residual, queries, fresh_rotated_keys, fresh_values, cache_keys, request_value_cache,
    cache_lengths, out_proj, router_weight, norm_gain, expert_ids, live_mask,
    w_gate, w_up, w_down,
):
    experts = router_weight.shape[1]
    core = lax.axis_index("dp").astype(jnp.int32).reshape(1)
    mine, other = attend(
        cache_lengths, core, queries, fresh_rotated_keys, fresh_values, cache_keys,
        request_value_cache, out_proj,
    )
    recv = lax.ppermute(other, "dp", [(0, 1), (1, 0)])
    base, chosen, rank, pick, last = prepare(
        residual, mine, expert_ids, live_mask.reshape(-1, 1), experts
    )
    hidden, gate, send = route(
        base, recv, router_weight, norm_gain.reshape(1, -1), chosen, pick, last
    )
    back = exchange(expert(exchange(send, experts), w_gate, w_up, w_down), experts)
    return combine(hidden, gate, rank, back)


def solution(mesh):
    both = ("ep", "dp")
    placed = (
        P(both, None),
        P("ep", "dp"),
        P("ep", "dp"),
        P("ep", "dp"),
        P("ep", None, "dp"),
        P("ep", None, "dp"),
        P("ep"),
        P("dp", None),
        P(),
        P(),
        P(both, None),
        P(both),
        P(both, None, None),
        P(both, None, None),
        P(both, None, None),
    )
    return jax.shard_map(
        on_device, mesh=mesh, in_specs=placed, out_specs=P(both, None), check_vma=False
    )
```

```python
import math

import jax
import jax.numpy as jnp
from jax import lax
from jax.experimental import pallas as pl
from jax.experimental.pallas import tpu as pltpu
from jax.sharding import PartitionSpec as P

HEAD = 128
NEG_FILL = -1e30
NORM_EPS = 1e-06
F32 = jnp.float32
BF16 = jnp.bfloat16
VMEM = pltpu.VMEM
LIMIT = 30 * 1024 * 1024
FULL = 52 * 1024 * 1024


def dot(a, b):
    return jnp.dot(a, b, preferred_element_type=F32)


def dot_nt(a, b):
    return lax.dot_general(a, b, (((1,), (1,)), ((), ())), preferred_element_type=F32)


def dot_tn(a, b):
    return lax.dot_general(a, b, (((0,), (0,)), ((), ())), preferred_element_type=F32)


def iota(shape, axis):
    return lax.broadcasted_iota(jnp.int32, shape, axis)


def softmax_parts(scores):
    top = jnp.max(scores, -1, keepdims=True)
    raised = jnp.exp(scores - top)
    return raised, jnp.sum(raised, -1, keepdims=True)


def attend_kernel(
    lens_ref, core_ref, q_hbm, fk_hbm, fv_hbm, ck_hbm, cv_hbm, wo_hbm,
    mine_hbm, other_hbm,
    q_ref, fk_ref, fv_ref, k_buf, v_buf, wo_buf, att, acc, dq, dk, dv, ds, do, sem,
):
    rows, width = q_ref.shape
    requests, slots, kvw = k_buf.shape
    decode = requests - 1
    span = rows - decode
    kvh = kvw // HEAD
    heads = width // HEAD
    per = heads // kvh
    scale = 1.0 / math.sqrt(HEAD)
    half = requests // 2 + 1

    cuts = ((0, 1), (1, half), (half, requests))
    copies = []
    for i, (lo, hi) in enumerate(cuts):
        copies.append(pltpu.make_async_copy(ck_hbm.at[pl.ds(lo, hi - lo)], k_buf.at[pl.ds(lo, hi - lo)], sem.at[0, i]))
        copies.append(pltpu.make_async_copy(cv_hbm.at[pl.ds(lo, hi - lo)], v_buf.at[pl.ds(lo, hi - lo)], sem.at[1, i]))
    pieces = 8
    step = wo_buf.shape[1] // pieces
    weights = [
        pltpu.make_async_copy(wo_hbm.at[:, pl.ds(i * step, step)], wo_buf.at[:, pl.ds(i * step, step)], sem.at[2, i])
        for i in range(pieces)
    ]
    small = [
        pltpu.make_async_copy(src, dst, sem.at[3, i])
        for i, (src, dst) in enumerate(((q_hbm, q_ref), (fk_hbm, fk_ref), (fv_hbm, fv_ref)))
    ]
    for c in small + copies + weights:
        c.start()
    for c in small:
        c.wait()

    tail = q_ref[span:, :].astype(F32)
    tail_k = fk_ref[span:, :].astype(F32)
    tail_v = fv_ref[span:, :].astype(F32)
    for h in range(heads):
        g = h // per
        dq[pl.ds(h, decode, stride=heads), :] = tail[:, h * HEAD : (h + 1) * HEAD]
        dk[pl.ds(h, decode, stride=heads), :] = tail_k[:, g * HEAD : (g + 1) * HEAD]
        dv[pl.ds(h, decode, stride=heads), :] = tail_v[:, g * HEAD : (g + 1) * HEAD]

    copies[0].wait()
    copies[1].wait()
    total = slots + span
    shape = (per * span, total)
    col = iota(shape, 1)
    place = iota(shape, 0) & (span - 1)
    allowed = ((col < slots) & (col < lens_ref[0])) | ((col >= slots) & (col - slots <= place))
    for g in range(kvh):
        gs = slice(g * HEAD, (g + 1) * HEAD)
        q = jnp.concatenate(
            [q_ref[:span, (g * per + j) * HEAD : (g * per + j + 1) * HEAD] for j in range(per)], 0
        )
        k = jnp.concatenate([k_buf[0, :, gs], fk_ref[:span, gs]], 0)
        v = jnp.concatenate([v_buf[0, :, gs], fv_ref[:span, gs]], 0)
        s = jnp.where(allowed, dot_nt(q, k) * scale, NEG_FILL)
        raised, norm = softmax_parts(s)
        p = (raised * (1.0 / norm)).astype(BF16)
        o = dot(p, v).astype(BF16)
        for j in range(per):
            h = g * per + j
            att[:span, h * HEAD : (h + 1) * HEAD] = o[j * span : (j + 1) * span]

    pairs = decode * heads
    lower = (iota((pairs, HEAD), 0) & (heads - 1)) < per
    qv = dq[...]
    qbd = jnp.concatenate([jnp.where(lower, qv, 0.0), jnp.where(lower, 0.0, qv)], 1).astype(BF16)
    own = jnp.sum(qv * dk[...], -1, keepdims=True) * scale
    lane = iota((heads, slots), 1)
    for r in range(decode):
        if r == 0:
            copies[2].wait()
        if r + 1 == half:
            copies[4].wait()
        s = dot_nt(qbd[r * heads : (r + 1) * heads], k_buf[r + 1]) * scale
        ds[r * heads : (r + 1) * heads, :] = jnp.where(lane < lens_ref[r + 1], s, NEG_FILL)
    s = ds[...]
    top = jnp.maximum(jnp.max(s, -1, keepdims=True), own)
    raised = jnp.exp(s - top)
    own_raised = jnp.exp(own - top)
    inv = 1.0 / (jnp.sum(raised, -1, keepdims=True) + own_raised)
    p = (raised * inv).astype(BF16)
    own_p = (own_raised * inv).astype(BF16).astype(F32)
    copies[3].wait()
    copies[5].wait()
    for r in range(decode):
        o = dot(p[r * heads : (r + 1) * heads], v_buf[r + 1])
        do[r * heads : r * heads + per, :] = o[:per, :HEAD]
        do[r * heads + per : (r + 1) * heads, :] = o[per:, HEAD:]
    do[...] = do[...] + own_p * dv[...]
    for h in range(heads):
        att[span:, h * HEAD : (h + 1) * HEAD] = do[pl.ds(h, decode, stride=heads), :].astype(BF16)

    own_rows = mine_hbm.shape[0]
    core = core_ref[0]
    first = pl.multiple_of(core * own_rows, 8)
    second = pl.multiple_of((1 - core) * own_rows, 8)
    a = att[...]
    leaving = []
    for i in range(pieces):
        weights[i].wait()
        cs = pl.ds(i * step, step)
        acc[:, cs] = dot(a, wo_buf[:, cs])
        for n, (at, dst) in enumerate(((second, other_hbm), (first, mine_hbm))):
            c = pltpu.make_async_copy(acc.at[pl.ds(at, own_rows), cs], dst.at[:, cs], sem.at[4 + n, i])
            c.start()
            leaving.append(c)
    for c in leaving:
        c.wait()


def attend(lens, core, q, fk, fv, ck, cv, wo):
    rows, width = q.shape
    requests, slots, kvw = ck.shape
    heads = width // HEAD
    pairs = (requests - 1) * heads
    own = rows // 2
    sm = pl.BlockSpec(memory_space=pltpu.SMEM)
    hb = pl.BlockSpec(memory_space=pl.ANY)
    out = jax.ShapeDtypeStruct((own, wo.shape[1]), F32)
    pinned = [pltpu.with_memory_space_constraint(a, pltpu.HBM) for a in (lens, q, fk, fv, ck, cv, wo)]
    return pl.pallas_call(
        attend_kernel,
        name="attend",
        out_shape=(out, out),
        in_specs=[sm, sm] + [hb] * 6,
        out_specs=(hb, hb),
        scratch_shapes=[
            VMEM(q.shape, BF16),
            VMEM(fk.shape, BF16),
            VMEM(fv.shape, BF16),
            VMEM(ck.shape, BF16),
            VMEM(cv.shape, BF16),
            VMEM(wo.shape, BF16),
            VMEM((rows, width), BF16),
            VMEM((rows, wo.shape[1]), F32),
            VMEM((pairs, HEAD), F32),
            VMEM((pairs, HEAD), F32),
            VMEM((pairs, HEAD), F32),
            VMEM((pairs, slots), F32),
            VMEM((pairs, HEAD), F32),
            pltpu.SemaphoreType.DMA((6, 8)),
        ],
        compiler_params=pltpu.CompilerParams(vmem_limit_bytes=FULL),
    )(pinned[0], core, *pinned[1:])


MAIN = 8


CHUNK = 288
GROUPS = 4
WINDOW = 128
MARK = 1e-36


def spread_last(scr, rows):
    tiles = scr.shape[0]
    for q in range(MAIN):
        for j in range(tiles):
            at = (q * tiles + j) * HEAD
            scr[j, pl.ds(q, rows.shape[0], stride=MAIN), :] = rows[:, at : at + HEAD]
    return jnp.concatenate([scr[j] for j in range(tiles)], 1).astype(BF16)


def collect_last(scr, pieces, count):
    tiles = scr.shape[0]
    pieces = pieces.astype(F32)
    for j in range(tiles):
        scr[j] = pieces[:, j * HEAD : (j + 1) * HEAD]
    rows = [scr[j, pl.ds(q, count, stride=MAIN), :] for q in range(MAIN) for j in range(tiles)]
    return jnp.concatenate(rows, 1).astype(BF16)


def last_scratch(rows, width):
    return VMEM((width // MAIN // HEAD, rows, HEAD), F32)


def expander(experts):
    shape = (experts, experts * MAIN)
    return ((iota(shape, 1) >> 3) == iota(shape, 0)).astype(F32).astype(BF16)


def prepare_kernel(
    res_ref, mine_ref, ids_ref, live_ref, router_hbm,
    base_ref, chosen_ref, rank_ref, pick_ref, last_ref, router_ref, sem,
):
    rows = res_ref.shape[0]
    experts = rank_ref.shape[1]
    load = pltpu.make_async_copy(router_hbm, router_ref, sem)
    load.start()
    base_ref[...] = res_ref[...].astype(F32) + mine_ref[...]
    lane = iota((rows, experts), 1)
    ids = ids_ref[...]
    chosen = ids[:, 0:1] == lane
    for k in range(1, ids.shape[1]):
        chosen = chosen | (ids[:, k : k + 1] == lane)
    chosen_ref[...] = jnp.where(chosen, 1.0, 0.0)
    used = jnp.where(chosen & (live_ref[...] > 0), 1.0, 0.0)
    before = (iota((rows, rows), 0) > iota((rows, rows), 1)).astype(F32).astype(BF16)
    rank = used * (dot(before, used.astype(BF16)) + 1.0)
    rank_ref[...] = rank
    spread = dot(rank.astype(BF16), expander(experts))
    slot = (iota(spread.shape, 1) & (MAIN - 1)).astype(F32) + 1.0
    pick_ref[...] = jnp.where(spread == slot, 1.0, 0.0).astype(BF16)
    last_ref[...] = jnp.where(rank == MAIN + 1.0, 1.0, 0.0).astype(BF16)
    load.wait()


def prepare(res, mine, ids, live, router):
    rows, width = res.shape
    experts = router.shape[1]
    res, router = [pltpu.with_memory_space_constraint(a, pltpu.HBM) for a in (res, router)]
    vm = pl.BlockSpec(memory_space=VMEM)
    return pl.pallas_call(
        prepare_kernel,
        name="prepare",
        out_shape=(
            jax.ShapeDtypeStruct((rows, width), F32),
            jax.ShapeDtypeStruct((rows, experts), F32),
            jax.ShapeDtypeStruct((rows, experts), F32),
            jax.ShapeDtypeStruct((rows, experts * MAIN), BF16),
            jax.ShapeDtypeStruct((rows, experts), BF16),
            jax.ShapeDtypeStruct(router.shape, BF16),
        ),
        in_specs=[vm] * 4 + [pl.BlockSpec(memory_space=pl.ANY)],
        out_specs=(vm,) * 6,
        scratch_shapes=[pltpu.SemaphoreType.DMA],
        cost_estimate=pl.CostEstimate(flops=2 * rows * width, bytes_accessed=10 * rows * width, transcendentals=0),
        compiler_params=pltpu.CompilerParams(vmem_limit_bytes=LIMIT),
    )(res, mine, ids, live, router)


def route_kernel(
    base_ref, recv_ref, router_ref, gain_ref, chosen_ref, pick_ref, last_ref,
    hidden_ref, gate_ref, send_ref, scr,
):
    width = base_ref.shape[1]
    hidden = (base_ref[...] + recv_ref[...]).astype(BF16)
    hidden_ref[...] = hidden
    h32 = hidden.astype(F32)
    mean = jnp.mean(h32 * h32, -1, keepdims=True)
    normed = (h32 * lax.rsqrt(mean + NORM_EPS) * gain_ref[...].astype(F32)).astype(BF16)
    head = normed[:, :HEAD].astype(F32)
    head = jnp.where((iota(head.shape, 1) == 0) & (head == 0.0), MARK, head).astype(BF16)
    marked = jnp.concatenate([head, normed[:, HEAD:]], 1)
    pick = pick_ref[...]
    block = width // 4
    for n in range(4):
        cs = slice(n * block, (n + 1) * block)
        send_ref[:, cs] = dot_tn(pick, marked[:, cs]).astype(BF16)
    send_ref[:, width:] = spread_last(scr, dot_tn(last_ref[...], marked))
    logits = dot(normed, router_ref[...])
    chosen = chosen_ref[...] > 0.0
    raised = jnp.where(chosen, jnp.exp(jnp.where(chosen, logits, 0.0)), 0.0)
    gate_ref[...] = raised / jnp.sum(raised, -1, keepdims=True)


def route(base, recv, router, gain, chosen, pick, last):
    rows, width = base.shape
    experts = router.shape[1]
    part = width // MAIN
    vm = pl.BlockSpec(memory_space=VMEM)
    return pl.pallas_call(
        route_kernel,
        name="route",
        out_shape=(
            jax.ShapeDtypeStruct((rows, width), BF16),
            jax.ShapeDtypeStruct((rows, experts), F32),
            jax.ShapeDtypeStruct((experts * MAIN, width + part), BF16),
        ),
        in_specs=[vm] * 7,
        out_specs=(vm,) * 3,
        scratch_shapes=[last_scratch(experts * MAIN, width)],
        compiler_params=pltpu.CompilerParams(vmem_limit_bytes=LIMIT),
    )(base, recv, router, gain, chosen, pick, last)


def in_use(rows):
    used = jnp.where((iota(rows.shape, 1) == 0) & (rows.astype(F32) != 0.0), 1.0, 0.0)
    return dot_nt(jnp.ones((8, HEAD), BF16), used.astype(BF16))


def places(main, last):
    sources = last.shape[1]
    grow = expander(sources)
    slot = iota(main.shape, 1) & (MAIN - 1)
    upto = main
    for shift in (1, 2, 4):
        upto = upto + jnp.where(slot >= shift, pltpu.roll(upto, shift, 1), 0.0)
    count = dot_nt(main.astype(BF16), grow)
    held = count + last
    before = (iota((sources, sources), 0) < iota((sources, sources), 1)).astype(F32).astype(BF16)
    base = dot(held.astype(BF16), before)
    high = jnp.floor(base * (1.0 / 64.0))
    parts = dot(jnp.concatenate([high, base - 64.0 * high], 0).astype(BF16), grow)
    first = 64.0 * parts[:8] + parts[8:]
    at_main = jnp.where(main > 0.0, first + upto - 1.0, -1.0)
    at_last = jnp.where(last > 0.0, base + count, -1.0)
    return at_main, at_last, base[0:1], jnp.sum(held[0:1]).astype(jnp.int32)


def expert_kernel(x_ref, wg_ref, wu_ref, wd_ref, y_ref, scr, x_buf, y_buf):
    wg, wu, wd = wg_ref.at[0], wu_ref.at[0], wd_ref.at[0]
    width = wg.shape[0]
    count = x_ref.shape[0]
    sources = count // MAIN
    last = collect_last(scr, x_ref[:, width:], sources)
    at_main, at_last, base, total = places(in_use(x_ref[:, :HEAD]), in_use(last[:, :HEAD]))
    block = width // 4
    members = sources // GROUPS
    lane = iota(base.shape, 1)
    edges = [
        jnp.sum(jnp.where(lane == j * members, base, 0.0)).astype(jnp.int32) for j in range(GROUPS)
    ] + [total]
    starts = [e & ~15 for e in edges[:-1]]
    fits = total <= CHUNK
    for j in range(GROUPS):
        fits = fits & (edges[j + 1] - starts[j] <= WINDOW)

    def mlp(x):
        g = dot(x, wg[...])
        u = dot(x, wu[...])
        return dot((g * jax.nn.sigmoid(g) * u).astype(BF16), wd[...])

    def hot(at, rows, start):
        row = iota((rows, at.shape[1]), 0) + start
        return jnp.where(at[0:1].astype(jnp.int32) == row, 1.0, 0.0).astype(BF16)

    @pl.when(fits)
    def _():
        main, tail = hot(at_main, CHUNK, 0), hot(at_last, CHUNK, 0)
        for n in range(4):
            cs = slice(n * block, (n + 1) * block)
            x_buf[:, cs] = (dot(main, x_ref[:, cs]) + dot(tail, last[:, cs])).astype(BF16)
        y_buf[:CHUNK, :] = mlp(x_buf[...]).astype(BF16)
        y_buf[CHUNK:, :] = jnp.zeros((WINDOW, width), BF16)
        size = members * MAIN
        for j in range(GROUPS):
            rows = slice(j * size, (j + 1) * size)
            near = hot(at_main[:, rows], WINDOW, starts[j])
            from_ = pl.ds(pl.multiple_of(starts[j], 16), WINDOW)
            for n in range(4):
                cs = slice(n * block, (n + 1) * block)
                y_ref[rows, cs] = dot_tn(near, y_buf[from_, cs]).astype(BF16)
        y_ref[:, width:] = spread_last(scr, dot_tn(tail, y_buf[:CHUNK, :]))

    @pl.when(jnp.logical_not(fits))
    def _():
        y_ref[:, width:] = spread_last(scr, mlp(last))
        step = 256

        @pl.loop(0, count // step)
        def _(i):
            rows = pl.ds(pl.multiple_of(i * step, step), step)
            y_ref[rows, :width] = mlp(x_ref[rows, :width]).astype(BF16)


def expert(x, wg, wu, wd):
    vm = pl.BlockSpec(memory_space=VMEM)
    width = wg.shape[1]
    return pl.pallas_call(
        expert_kernel,
        name="expert",
        out_shape=jax.ShapeDtypeStruct(x.shape, BF16),
        in_specs=[vm] * 4,
        out_specs=vm,
        scratch_shapes=[
            last_scratch(x.shape[0], width),
            VMEM((CHUNK, width), BF16),
            VMEM((CHUNK + WINDOW, width), BF16),
        ],
        compiler_params=pltpu.CompilerParams(vmem_limit_bytes=LIMIT),
    )(x, wg, wu, wd)


def combine_kernel(hidden_ref, gate_ref, rank_ref, y_ref, out_ref, scr):
    rows, width = hidden_ref.shape
    experts = gate_ref.shape[1]
    rank = rank_ref[...]
    gate = gate_ref[...]
    high = gate.astype(BF16).astype(F32)
    both = jnp.concatenate([high, gate - high], 0)
    rank2 = jnp.concatenate([rank, rank], 0)
    grow = expander(experts)
    spread = dot(rank2.astype(BF16), grow)
    slot = (iota(spread.shape, 1) & (MAIN - 1)).astype(F32) + 1.0
    main = jnp.where(spread == slot, dot(both.astype(BF16), grow), 0.0).astype(BF16)
    last = jnp.where(rank2 == MAIN + 1.0, both, 0.0).astype(BF16)
    tail = collect_last(scr, y_ref[:, width:], experts)
    block = width // 4
    for n in range(4):
        cs = slice(n * block, (n + 1) * block)
        mix = dot(main, y_ref[:, cs]) + dot(last, tail[:, cs])
        out_ref[:, cs] = (hidden_ref[:, cs].astype(F32) + (mix[:rows] + mix[rows:])).astype(BF16)


def combine(hidden, gate, rank, y):
    vm = pl.BlockSpec(memory_space=VMEM)
    return pl.pallas_call(
        combine_kernel,
        name="combine",
        out_shape=jax.ShapeDtypeStruct(hidden.shape, BF16),
        in_specs=[vm] * 4,
        out_specs=vm,
        scratch_shapes=[last_scratch(y.shape[0], hidden.shape[1])],
        compiler_params=pltpu.CompilerParams(vmem_limit_bytes=LIMIT),
    )(hidden, gate, rank, y)


def exchange(x, experts):
    blocks = x.reshape(experts, MAIN, x.shape[1])
    moved = lax.all_to_all(blocks, ("ep", "dp"), split_axis=0, concat_axis=0, tiled=True)
    return moved.reshape(x.shape)


def on_device(
    residual, queries, fresh_rotated_keys, fresh_values, cache_keys, request_value_cache,
    cache_lengths, out_proj, router_weight, norm_gain, expert_ids, live_mask,
    w_gate, w_up, w_down,
):
    experts = router_weight.shape[1]
    core = lax.axis_index("dp").astype(jnp.int32).reshape(1)
    mine, other = attend(
        cache_lengths, core, queries, fresh_rotated_keys, fresh_values, cache_keys,
        request_value_cache, out_proj,
    )
    recv = lax.ppermute(other, "dp", [(0, 1), (1, 0)])
    base, chosen, rank, pick, last, router_here = prepare(
        residual, mine, expert_ids, live_mask.reshape(-1, 1), router_weight
    )
    hidden, gate, send = route(
        base, recv, router_here, norm_gain.reshape(1, -1), chosen, pick, last
    )
    back = exchange(expert(exchange(send, experts), w_gate, w_up, w_down), experts)
    return combine(hidden, gate, rank, back)


def solution(mesh):
    both = ("ep", "dp")
    placed = (
        P(both, None),
        P("ep", "dp"),
        P("ep", "dp"),
        P("ep", "dp"),
        P("ep", None, "dp"),
        P("ep", None, "dp"),
        P("ep"),
        P("dp", None),
        P(),
        P(),
        P(both, None),
        P(both),
        P(both, None, None),
        P(both, None, None),
        P(both, None, None),
    )
    return jax.shard_map(
        on_device, mesh=mesh, in_specs=placed, out_specs=P(both, None), check_vma=False
    )
```
